512 devices in a mesh: dp: 16 (over x, y_hi), ep: 32 (over y_lo, z, core).
Axes of the slice: x: 4, y: 8 (y_hi: 4, y_lo: 2; y = y_hi * 2 + y_lo), z: 8, core: 2. Of those that a mesh axis runs over, the one named last changes fastest.
Arguments:
- tokens: bfloat16 [65536, 2048], P(('dp', 'ep')), may hold values from -6 to 6
- cotangent: bfloat16 [65536, 2048], P(('dp', 'ep')), may hold values from -6 to 6
- expert_ids: int32 [65536, 8], P(('dp', 'ep')), may hold values from 0 to 31, all different within a row; in each aligned block of 128 rows (0 to 127, 128 to 255, ...) at most 34 rows name the same one
- gate_weights: bfloat16 [65536, 8], P(('dp', 'ep')), may hold values from 0.019897461 to 0.3984375
- w_up: bfloat16 [32, 2048, 384], P('ep'), may hold values from -0.125 to 0.125
- w_down: bfloat16 [32, 2048, 384], P('ep'), may hold values from -0.3125 to 0.3125
Outputs:
- token_grad: bfloat16 [65536, 2048], P(('dp', 'ep'))
- gate_grad: bfloat16 [65536, 8], P(('dp', 'ep'))
- down_grad: float32 [32, 2048, 384], P('ep', 'dp')
The draws below stay inside these ranges and needn't reach their ends.
Inputs may be any that keep to these rules, and one draw needn't show every extreme that they name: `expert_ids`: each token names 8 different experts; among the 128 tokens of one device (aligned blocks of rows) no expert is named more than 34 times, and in some block one expert is named exactly 34 times.
All inputs are finite; a program needn't handle non-finite values.
Results may differ from the reference program's by a relative error of at most 0.008.
Values may be sent and summed in bfloat16 or wider, within the bound.
A program may use at most 128 MiB of HBM per device.

```python
import math
import jax
import jax.numpy as jnp
import numpy as np
from jax import lax

D = 2048
H = 384
TOPK = 8
TOK_DEV = 128
EXPERTS = 32
CAP = 34
TOKENS = 65536


def strengthened(values, key, source, target, blocks, factor):
    owner, partner = [(jnp.arange(values.shape[position]) // (values.shape[position] // blocks)).reshape([-1 if axis == position else 1 for axis in range(values.ndim)]) for position in (source, target)]
    chosen = jax.random.permutation(key, blocks)[partner]
    strong = (owner == chosen) | (owner == (partner + blocks // 2) % blocks)
    return jnp.where(strong, factor * values, values)


def block_levels(key, dims, shards, least, high):
    level, own = 1.0, jax.random.fold_in(key, 6)
    for dim, blocks in shards:
        steps = jnp.exp(jax.random.uniform(jax.random.fold_in(own, dim), (blocks,), jnp.float32, least / len(shards), high / len(shards)))
        level = level * jnp.repeat(steps, dims[dim] // blocks).reshape([-1 if axis == dim else 1 for axis in range(len(dims))])
    return level


def assign_block(key, own, number, rows, amount, top, limit, skew):
    ranking = jax.random.permutation(key, amount)
    packed, common = load_shares(amount, rows * top, limit, skew, True), load_shares(amount, rows * top, limit, skew, False)
    places = jnp.arange(amount)

    def named(lengths, offset_by):
        used = int((lengths > 0).sum())
        fixed = max(1, used // 4)
        shifted = fixed + (places - fixed + offset_by * (used - fixed)) % max(1, amount - fixed)
        return jnp.zeros((amount,), jnp.int32).at[ranking[jnp.where(places < fixed, places, shifted)]].set(jnp.asarray(lengths, jnp.int32))

    lengths = jnp.where(number % 4 == 0, named(packed, number // 4), named(common, number - number // 4 - 1))
    mixed = jax.random.permutation(jax.random.fold_in(own, 3), amount)
    source_of, sink = mixed[0:amount // 2 * 2:2], mixed[1:amount // 2 * 2:2]
    margin = jnp.minimum(lengths[source_of] - 1, limit - lengths[sink]) // 2
    margin = jnp.where((source_of == ranking[0]) | (sink == ranking[0]) | (lengths[sink] == 0), 0, jnp.maximum(margin, 0))
    shifted = jax.random.randint(jax.random.fold_in(own, 4), (amount // 2,), 0, 1 << 20) % (margin + 1)
    lengths = lengths.at[source_of].add(-shifted).at[sink].add(shifted)
    items = jnp.searchsorted(jnp.cumsum(lengths), jnp.arange(rows * top), side="right").astype(jnp.int32)
    table = items.reshape(top, rows).T
    table = table[jax.random.permutation(jax.random.fold_in(own, 1), rows)]
    offset_by = jax.random.randint(jax.random.fold_in(own, 2), (rows, 1), 0, top)
    return jnp.take_along_axis(table, (jnp.arange(top)[None, :] + offset_by) % top, axis=1)


def load_shares(amount, total, reach, skew, full):
    weights = [(1 << 20) // math.isqrt(rank ** skew) + 1 for rank in range(1, amount + 1)]
    largest = reach if full else min(reach, max(-(-total // amount), total * weights[0] // sum(weights)))
    least = 1 if total - largest >= amount - 1 else 0
    holding, surplus = [largest] + [least] * (amount - 1), total - largest - least * (amount - 1)
    while surplus > 0:
        candidates = [i for i in range(1, amount) if holding[i] < largest] or [i for i in range(1, amount) if holding[i] < reach]
        mass, left = sum([weights[i] for i in candidates]), surplus
        for i in candidates:
            extra = min(reach - holding[i], max(1, left * weights[i] // mass), surplus)
            holding[i] = holding[i] + extra
            surplus = surplus - extra
    return np.array(holding)


def noise(stream_key, extent, scale, reach, split=(), held_as=jnp.bfloat16):
    entries = jax.random.normal(stream_key, extent, jnp.float32) * scale
    if len(split) > 0:
        entries = block_levels(stream_key, extent, split, -0.22, 0.18) * entries
    return jnp.clip(entries, min=-reach, max=reach).astype(held_as)


def gaussian_with(key, extent, deviation, bound, cuts, heavy, held_as=jnp.bfloat16):
    entries = deviation * jax.random.normal(key, extent, jnp.float32)
    if cuts:
        entries = entries * block_levels(key, extent, cuts, -0.22, 0.18)
    return jnp.clip(strengthened(entries, jax.random.fold_in(key, 3), *heavy), -bound, bound).astype(held_as)


def setup_inputs(seed: int = 0) -> dict:
    streams_of = jax.random.split(jax.random.key(seed), 7)
    tokens = noise(streams_of[0], (TOKENS, D), 1.0, 6.0, ((0, 512),))
    cotangent = gaussian_with(streams_of[1], (TOKENS, D), 0.3, 6.0, ((0, 512),), (0, 1, 512, 6.0))
    expert_ids_keys = jax.random.split(jax.random.fold_in(streams_of[2], 1), TOKENS // TOK_DEV)
    expert_ids_turns = jax.random.permutation(jax.random.fold_in(streams_of[2], 3), TOKENS // TOK_DEV)
    expert_ids = jax.vmap(lambda own, number: assign_block(jax.random.fold_in(streams_of[2], 2), own, number, TOK_DEV, EXPERTS, TOPK, CAP, 0))(expert_ids_keys, expert_ids_turns).reshape((TOKENS, TOPK))
    gate_weights = jnp.clip(jnp.exp(math.log(0.3984375) - 2.9969585 * jax.random.uniform(streams_of[3], (TOKENS, TOPK), jnp.float32) ** block_levels(streams_of[3], (TOKENS, TOPK), ((0, 512),), -0.2, 0.2)), 0.019897461, 0.3984375).astype(jnp.bfloat16)
    w_up = noise(streams_of[4], (EXPERTS, D, H), D ** -0.5, 0.125, ((0, 32),))
    w_down = noise(streams_of[5], (EXPERTS, D, H), H ** -0.5, 0.3125, ((0, 32),))
    return dict(tokens=tokens, cotangent=cotangent, expert_ids=expert_ids, gate_weights=gate_weights, w_up=w_up, w_down=w_down)


def reference(tokens, cotangent, expert_ids, gate_weights, w_up, w_down):
    route_total = TOKENS * TOPK
    block_count = TOKENS // TOK_DEV
    block_routes = TOK_DEV * TOPK
    ids = expert_ids.reshape(block_count, block_routes)
    table = (ids[:, :, None] == jnp.arange(EXPERTS, dtype=jnp.int32)[None, None, :]).astype(jnp.int32)
    earlier = jnp.sum(jnp.cumsum(table, axis=1) * table, axis=2) - 1
    block_of = jnp.arange(block_count, dtype=jnp.int32)[:, None]
    global_pos = ((ids * block_count + block_of) * CAP + earlier).astype(jnp.int32)
    region = block_count * CAP
    inverse = jnp.full((EXPERTS * region,), route_total, jnp.int32)
    inverse = inverse.at[global_pos.reshape(route_total)].set(jnp.arange(route_total, dtype=jnp.int32))
    inverse = inverse.reshape(EXPERTS, region)
    flat_gates = gate_weights.reshape(route_total)

    def one_expert(carry, inputs):
        grad_acc, gate_acc = carry
        rows_inv, up_matrix, down_matrix = inputs
        occupied = rows_inv < route_total
        route_of = jnp.minimum(rows_inv, route_total - 1)
        token_of = route_of // TOPK
        x_rows = jnp.where(occupied[:, None], tokens[token_of], jnp.zeros((), tokens.dtype))
        dy_rows = jnp.where(occupied[:, None], cotangent[token_of], jnp.zeros((), cotangent.dtype))
        gate_f = jnp.where(occupied, flat_gates[route_of], jnp.zeros((), flat_gates.dtype)).astype(jnp.float32)
        pre_act = jnp.dot(x_rows, up_matrix, preferred_element_type=jnp.float32)
        hidden = jax.nn.silu(pre_act).astype(jnp.bfloat16)
        back_hidden = jnp.dot(dy_rows, down_matrix, preferred_element_type=jnp.float32)
        gate_rows = jnp.sum(back_hidden * hidden.astype(jnp.float32), axis=1).astype(jnp.bfloat16)
        sig = jax.nn.sigmoid(pre_act)
        slope = sig * (1.0 + pre_act * (1.0 - sig))
        grad_pre = (gate_f[:, None] * back_hidden * slope).astype(jnp.bfloat16)
        route_grad = jnp.dot(grad_pre, up_matrix.T, preferred_element_type=jnp.float32).astype(jnp.bfloat16)
        scaled_cot = (gate_f[:, None] * dy_rows.astype(jnp.float32)).astype(jnp.bfloat16)
        down_part = jnp.dot(scaled_cot.T, hidden, preferred_element_type=jnp.float32)
        grad_acc = grad_acc.at[token_of].add(jnp.where(occupied[:, None], route_grad.astype(jnp.float32), jnp.zeros((), jnp.float32)))
        gate_acc = gate_acc.at[route_of].add(jnp.where(occupied, gate_rows.astype(jnp.float32), jnp.zeros((), jnp.float32)))
        return (grad_acc, gate_acc), down_part

    start_carry = (jnp.zeros((TOKENS, D), jnp.float32), jnp.zeros((route_total,), jnp.float32))
    (grad_acc, gate_acc), down_grad = lax.scan(one_expert, start_carry, (inverse, w_up, w_down))
    token_grad = grad_acc.astype(jnp.bfloat16)
    gate_grad = gate_acc.reshape(TOKENS, TOPK).astype(jnp.bfloat16)
    return (token_grad, gate_grad, down_grad)
```

```python
import jax
import jax.numpy as jnp
from jax import lax
from jax.experimental import pallas as pl
from jax.experimental.pallas import tpu as pltpu
from jax.sharding import PartitionSpec as P

MESH = pl.DeviceIdType.MESH
BF16, F32 = jnp.bfloat16, jnp.float32
NX, NYH, NZ = 4, 4, 8
NY = 2 * NYH
ROWS = 128
LANES = 128
HALF = 1024


def kernel(
    xg_ref, dy_ref, wu_ref, wd_ref, tok_ref, gg_ref, dg_ref,
    xb, db, wu, wd, gh, gp, pre_s, bh_s, pb, rb, dyt, a_s, s_s, r_s, x1, x2, yr,
    loc_sem, ag_send, ag_recv, w_send, w_recv, rs_send, rs_recv, c_send, c_recv, x_send, x_recv, y_send, y_recv,
):
    width = dy_ref.shape[1]
    hid_n = wu_ref.shape[2]
    wide = xg_ref.shape[1]
    dp, ep = lax.axis_index("dp"), lax.axis_index("ep")
    core = lax.rem(ep, 2)
    z = lax.rem(ep // 2, NZ)
    yl = ep // (2 * NZ)
    x, yh = dp // NYH, lax.rem(dp, NYH)
    yy = 2 * yh + yl

    def dev(x_, y_, z_, c_):
        return (x_ * NYH + y_ // 2, (lax.rem(y_, 2) * NZ + z_) * 2 + c_)

    zdev = [dev(x, yy, lax.rem(z + 1, NZ), core), dev(x, yy, lax.rem(z + NZ - 1, NZ), core)]
    cdev = dev(x, yy, z, 1 - core)
    ydev = [None] + [dev(x, lax.rem(yy + d, NY), z, core) for d in range(1, NY)]
    y_pair = dev(x, lax.rem(yy + NY + 1 - 2 * yl, NY), z, core)
    y_other = dev(x, lax.rem(yy + NY + 2 * yl - 1, NY), z, core)
    xdev = [dev(lax.rem(x + 1, NX), yy, z, core), dev(lax.rem(x + NX - 1, NX), yy, z, core)]

    barrier = pltpu.get_barrier_semaphore()
    partners = zdev + [cdev] + ydev[1:] + xdev
    for device in partners:
        pl.semaphore_signal(barrier, inc=1, device_id=device, device_id_type=MESH)

    own = [
        pltpu.make_async_copy(xg_ref, xb.at[pl.ds(0, ROWS)], loc_sem.at[0]),
        pltpu.make_async_copy(dy_ref, db.at[pl.ds(0, ROWS)], loc_sem.at[1]),
        pltpu.make_async_copy(wu_ref.at[0], wu.at[0], loc_sem.at[2]),
        pltpu.make_async_copy(wd_ref.at[0], wd.at[0], loc_sem.at[3]),
    ]
    for copy in own:
        copy.start()
    pl.semaphore_wait(barrier, len(partners))

    def remote(src, dst, ssem, rsem, device):
        return pltpu.make_async_remote_copy(
            src_ref=src, dst_ref=dst, send_sem=ssem, recv_sem=rsem,
            device_id=device, device_id_type=MESH,
        )

    bufs = (xb, db)

    def block(arr, start):
        return bufs[arr].at[pl.ds(pl.multiple_of(start, ROWS), ROWS)]

    for arr, src in enumerate((xg_ref, dy_ref)):
        for r in range(2):
            remote(
                src, block(arr, (2 + r) * ROWS), ag_send.at[arr, r, 0], ag_recv.at[arr, r, 1], zdev[r]
            ).start()
    part = width // 2
    weight_first = []
    for m, (src, buf, far) in enumerate(((wu_ref, wu, y_pair), (wd_ref, wd, y_other))):
        for h in range(2):
            rows = pl.ds(h * part, part)
            weight_first.append(remote(
                src.at[0, rows], buf.at[2, rows], w_send.at[m, h, 0], w_recv.at[m, h, 0], far))
    for copy in weight_first:
        copy.start()
    weight_core = []
    for m, (src, buf) in enumerate(((wu_ref, wu), (wd_ref, wd))):
        for h in range(2):
            rows = pl.ds(h * part, part)
            weight_core.append(remote(
                src.at[0, rows], buf.at[1, rows], w_send.at[m, h, 1], w_recv.at[m, h, 1], cdev))
    for copy in weight_core:
        copy.start()
    weight_relay = []
    for m, buf in enumerate((wu, wd)):
        for h in range(2):
            rows = pl.ds(h * part, part)
            weight_relay.append(remote(
                buf.at[2, rows], buf.at[3, rows], w_send.at[m, h, 2], w_recv.at[m, h, 2], cdev))

    def ring_row(s, r):
        return jnp.where(s == 4, ROWS, (2 * s + r) * ROWS)

    lane = lax.broadcasted_iota(jnp.int32, (1, LANES), 1)
    chunk = 32

    def ring_step(i, carry):
        s = i + 1
        for arr in range(2):
            for r in range(2):
                def arrive(arr=arr, r=r):
                    here = block(arr, ring_row(s, r))
                    remote(here, here, ag_send.at[arr, r, 0], ag_recv.at[arr, r, s], zdev[r]).wait_recv()

                    @pl.when(s <= (3 if arr == r else 2))
                    def _():
                        remote(
                            here, block(arr, ring_row(s + 1, r)),
                            ag_send.at[arr, r, s], ag_recv.at[arr, r, s + 1], zdev[r],
                        ).start()

                if arr == r:
                    arrive()
                else:
                    pl.when(s <= 3)(arrive)

        @pl.when(i == 0)
        def _():
            for h in range(2):
                for m in range(2):
                    weight_first[2 * m + h].wait_recv()
                    weight_relay[2 * m + h].start()
            for copy in weight_core:
                copy.wait_recv()
            for copy in own:
                copy.wait()
            for copy in weight_relay:
                copy.wait_recv()

        base = pl.multiple_of(jnp.where(i == 3, 0, (i + 1) * 2 * ROWS), 2 * ROWS)
        rows = pl.ds(base, 2 * ROWS)
        pb[rows, width:] = jnp.zeros((2 * ROWS, LANES), BF16)

        def expert(j, carry):
            yl_j = jnp.where(j < 2, yl, 1 - yl)
            c_j = jnp.where(lax.rem(j, 2) == 0, core, 1 - core)
            e = (yl_j * NZ + z) * 2 + c_j
            pre_s[...] = jnp.dot(xb[rows, :width], wu[j], preferred_element_type=F32)
            bh_s[...] = jnp.dot(db[rows, :], wd[j], preferred_element_type=F32)

            def piece(q, carry):
                at = pl.multiple_of(q * chunk, chunk)
                sub = pl.ds(at, chunk)
                big = pl.ds(pl.multiple_of(base + at, chunk), chunk)
                mine = lane == e
                g = jnp.sum(jnp.where(mine, xb[big, width:].astype(F32), 0.0), axis=1, keepdims=True)
                pre, bh = pre_s[sub, :], bh_s[sub, :]
                sig = 0.5 * jnp.tanh(0.5 * pre) + 0.5
                hidden = (pre * sig).astype(BF16).astype(F32)
                gate = jnp.sum(bh * hidden, axis=1, keepdims=True)
                slope = sig * (1.0 + pre * (1.0 - sig))
                gp[j, sub, :] = (g * bh * slope).astype(BF16)
                gh[j, big, :] = (g * hidden).astype(BF16)
                pb[big, width:] = jnp.where(mine, gate, pb[big, width:].astype(F32)).astype(BF16)
                return carry

            return lax.fori_loop(0, 2 * ROWS // chunk, piece, carry)

        lax.fori_loop(0, 4, expert, 0)

        def columns(t, carry):
            at = pl.ds(pl.multiple_of(t * 512, 512), 512)
            total = None
            for j in range(4):
                term = lax.dot_general(
                    gp[j], wu[j, at, :], (((1,), (1,)), ((), ())), preferred_element_type=F32)
                total = term if total is None else total + term
            pb[rows, at] = total.astype(BF16)
            return carry

        lax.fori_loop(0, width // 512, columns, 0)
        return carry

    lax.fori_loop(0, 4, ring_step, 0)

    cols = (pl.ds(0, HALF), pl.ds(HALF, wide - HALF))
    back = (zdev[1], zdev[0])

    def rs_copy(r, t, h):
        row = ROWS if t == 0 else (2 * (4 - t) + r) * ROWS
        return remote(
            pb.at[pl.ds(row, ROWS), cols[h]], rb.at[r, t, :, cols[h]],
            rs_send.at[r, t, h], rs_recv.at[r, t, h], back[r])

    for r in range(2):
        rs_copy(r, 0, r).start()
    for r in range(2):
        rs_copy(r, 1, 1 - r).start()

    def rs_step(t):
        order = [(r, h) for h in ((0, 1)) for r in range(2)]
        order = [(r, r ^ k) for k in ((1, 0)) for r in range(2)] if t > 1 else [(r, r) for r in range(2)]
        for r, h in order:
            rs_copy(r, t - 1, h).wait_recv()
            row = pl.ds((2 * (4 - t) + r) * ROWS, ROWS)
            pb[row, cols[h]] = (
                pb[row, cols[h]].astype(F32) + rb[r, t - 1, :, cols[h]].astype(F32)).astype(BF16)
            rs_copy(r, t, h).start()

    tile = width // NX

    def down_tile(q, carry):
        d = jnp.where(q == 0, 2, jnp.where(q == 3, 0, jnp.where(q == 2, 3, 1)))
        at = pl.ds(pl.multiple_of(lax.rem(x + d, NX) * tile, tile), tile)

        def flip(k, carry):
            sub = pl.ds(pl.multiple_of(k * ROWS, ROWS), ROWS)
            dyt[:, sub] = db[sub, at].T
            return carry

        lax.fori_loop(0, NZ, flip, 0)

        def pair(jj, carry):
            s_s[q, jj] = jnp.dot(dyt[...], gh[2 * jj + 1], preferred_element_type=F32).astype(BF16)
            a_s[q, jj] = jnp.dot(dyt[...], gh[2 * jj], preferred_element_type=F32).astype(BF16)
            return carry

        lax.fori_loop(0, 2, pair, 0)
        remote(s_s.at[q], r_s.at[q], c_send.at[q], c_recv.at[q], cdev).start()
        return carry

    lax.fori_loop(0, NX, down_tile, 0)
    rs_step(1)

    def core_copy(q):
        return remote(s_s.at[q], r_s.at[q], c_send.at[q], c_recv.at[q], cdev)

    def add_into(dst, *others):
        total = dst[...].astype(F32)
        for other in others:
            total = total + other[...].astype(F32)
        dst[...] = total.astype(BF16)

    def x_first(r):
        return remote(a_s.at[0, r], x1.at[r], x_send.at[0, r], x_recv.at[0, r], xdev[r])

    def x_second(r):
        return remote(a_s.at[1 + r], x2.at[r], x_send.at[1, r], x_recv.at[1, r], xdev[r])

    core_copy(0).wait_recv()
    for jj in range(2):
        add_into(a_s.at[0, jj], r_s.at[0, jj])
    for r in range(2):
        x_first(r).start()
    for q in (1, 2, 3):
        core_copy(q).wait_recv()
        for jj in range(2):
            add_into(a_s.at[q, jj], r_s.at[q, jj])
    rs_step(2)
    for r in range(2):
        x_first(r).wait_recv()
        add_into(a_s.at[1 + r, r], x1.at[r])
        x_second(r).start()
    rs_step(3)
    for r in range(2):
        x_second(r).wait_recv()
    for jj in range(2):
        add_into(a_s.at[3, jj], x2.at[0, jj], x2.at[1, jj])

    def y_copy(d):
        row = pl.multiple_of((lax.rem(yy + d, NY) // 2) * ROWS, ROWS)
        return remote(
            a_s.at[3, d % 2, pl.ds(row, ROWS)], yr.at[d - 1], y_send.at[d - 1], y_recv.at[d - 1], ydev[d])

    for d in range(1, NY):
        y_copy(d).start()

    for r in range(2):
        for h in range(2):
            rs_copy(r, 3, h).wait_recv()
    first = pl.ds(0, ROWS)
    final = pb[first, :].astype(F32) + rb[0, 3].astype(F32) + rb[1, 3].astype(F32)
    tok_ref[...] = final[:, :width].astype(BF16)
    gg_ref[...] = final[:, width:].astype(BF16)

    total = a_s[3, 0, pl.ds(pl.multiple_of(yh * ROWS, ROWS), ROWS), :].astype(F32)
    for d in range(1, NY):
        y_copy(d).wait_recv()
        total = total + yr[d - 1].astype(F32)
    dg_ref[...] = total

    for arr in range(2):
        for r in range(2):
            for s in range(4 if arr == r else 3):
                here = block(arr, 0)
                remote(here, here, ag_send.at[arr, r, s], ag_recv.at[arr, r, 1], zdev[r]).wait_send()
    for copy in weight_first + weight_core + weight_relay:
        copy.wait_send()
    for r in range(2):
        rs_copy(r, 0, r).wait_send()
        for t in range(1, 4):
            for h in range(2):
                rs_copy(r, t, h).wait_send()
        x_first(r).wait_send()
        x_second(r).wait_send()
    for q in range(NX):
        core_copy(q).wait_send()
    for d in range(1, NY):
        y_copy(d).wait_send()


def shards(tokens, cotangent, expert_ids, gate_weights, w_up, w_down):
    rows, width = tokens.shape
    hid_n = w_up.shape[2]
    wide = width + LANES
    experts = jnp.arange(LANES, dtype=jnp.int32)
    hits = expert_ids[:, :, None] == experts[None, None, :]
    dense = jnp.sum(jnp.where(hits, gate_weights.astype(F32)[:, :, None], 0.0), axis=1).astype(BF16)
    xg = jnp.concatenate([tokens, dense], axis=1)
    tile = width // NX
    dma, vmem = pltpu.SemaphoreType.DMA, pltpu.VMEM
    hbm = pl.BlockSpec(memory_space=pl.ANY)
    token_grad, gates, down = pl.pallas_call(
        kernel,
        out_shape=(
            jax.ShapeDtypeStruct((rows, width), BF16),
            jax.ShapeDtypeStruct((rows, LANES), BF16),
            jax.ShapeDtypeStruct((width // (NX * NYH), hid_n), F32),
        ),
        in_specs=[hbm] * 4,
        out_specs=[pl.BlockSpec(memory_space=pltpu.VMEM)] * 3,
        scratch_shapes=[
            vmem((NZ * rows, wide), BF16),
            vmem((NZ * rows, width), BF16),
            vmem((4, width, hid_n), BF16),
            vmem((4, width, hid_n), BF16),
            vmem((4, NZ * rows, hid_n), BF16),
            vmem((4, 2 * rows, hid_n), BF16),
            vmem((2 * rows, hid_n), F32),
            vmem((2 * rows, hid_n), F32),
            vmem((NZ * rows, wide), BF16),
            vmem((2, 4, rows, wide), BF16),
            vmem((tile, NZ * rows), BF16),
            vmem((NX, 2, tile, hid_n), BF16),
            vmem((NX, 2, tile, hid_n), BF16),
            vmem((NX, 2, tile, hid_n), BF16),
            vmem((2, tile, hid_n), BF16),
            vmem((2, 2, tile, hid_n), BF16),
            vmem((NY - 1, rows, hid_n), BF16),
            dma((4,)),
            dma((2, 2, 4)),
            dma((2, 2, 5)),
            dma((2, 2, 3)),
            dma((2, 2, 3)),
            dma((2, 4, 2)),
            dma((2, 4, 2)),
            dma((NX,)),
            dma((NX,)),
            dma((2, 2)),
            dma((2, 2)),
            dma((NY - 1,)),
            dma((NY - 1,)),
        ],
        compiler_params=pltpu.CompilerParams(
            collective_id=0, has_side_effects=True, vmem_limit_bytes=66_000_000
        ),
        name="expert_backward",
    )(xg, cotangent, w_up, w_down)
    picked = jnp.where(hits, gates.astype(F32)[:, None, :], 0.0)
    gate_grad = jnp.sum(picked, axis=2).astype(BF16)
    return token_grad, gate_grad, down[None]


def solution(mesh):
    return jax.shard_map(
        shards,
        mesh=mesh,
        in_specs=(
            P(("dp", "ep"), None),
            P(("dp", "ep"), None),
            P(("dp", "ep"), None),
            P(("dp", "ep"), None),
            P("ep", None, None),
            P("ep", None, None),
        ),
        out_specs=(P(("dp", "ep"), None), P(("dp", "ep"), None), P("ep", "dp", None)),
        check_vma=False,
    )
```

```python
import jax
import jax.numpy as jnp
from jax import lax
from jax.experimental import pallas as pl
from jax.experimental.pallas import tpu as pltpu
from jax.sharding import PartitionSpec as P

MESH = pl.DeviceIdType.MESH
BF16, F32 = jnp.bfloat16, jnp.float32
NX, NYH, NZ = 4, 4, 8
NY = 2 * NYH
ROWS = 128
LANES = 128
HALF = 1024
EXP = 32


def kernel(
    x_ref, dy_ref, wu_ref, wd_ref, ids_ref, gates_ref, tok_ref, gg_ref, dg_ref,
    xb, db, gt, wu, wd, gh, gp, pre_s, bh_s, gs, gq, pb, pg, rb, rg, dyt, a_s, s_s, r_s, x1, x2, yr,
    loc_sem, ag_send, ag_recv, w_send, w_recv, rs_send, rs_recv, c_send, c_recv, x_send, x_recv, y_send, y_recv,
):
    width = dy_ref.shape[1]
    hid_n = wu_ref.shape[2]
    tile = width // NX
    dp, ep = lax.axis_index("dp"), lax.axis_index("ep")
    core = lax.rem(ep, 2)
    z = lax.rem(ep // 2, NZ)
    yl = ep // (2 * NZ)
    x, yh = dp // NYH, lax.rem(dp, NYH)
    yy = 2 * yh + yl

    def dev(x_, y_, z_, c_):
        return (x_ * NYH + y_ // 2, (lax.rem(y_, 2) * NZ + z_) * 2 + c_)

    zdev = [dev(x, yy, lax.rem(z + 1, NZ), core), dev(x, yy, lax.rem(z + NZ - 1, NZ), core)]
    cdev = dev(x, yy, z, 1 - core)
    ydev = [None] + [dev(x, lax.rem(yy + d, NY), z, core) for d in range(1, NY)]
    y_pair = dev(x, lax.rem(yy + NY + 1 - 2 * yl, NY), z, core)
    y_other = dev(x, lax.rem(yy + NY + 2 * yl - 1, NY), z, core)
    xdev = [dev(lax.rem(x + 1, NX), yy, z, core), dev(lax.rem(x + NX - 1, NX), yy, z, core)]

    barrier = pltpu.get_barrier_semaphore()
    partners = zdev + [cdev] + ydev[1:] + xdev
    for device in partners:
        pl.semaphore_signal(barrier, inc=1, device_id=device, device_id_type=MESH)

    OWN, FAR = (NZ - 2) * ROWS, (NZ - 1) * ROWS
    own = [
        pltpu.make_async_copy(x_ref, xb.at[pl.ds(OWN, ROWS)], loc_sem.at[0]),
        pltpu.make_async_copy(dy_ref, db.at[pl.ds(OWN, ROWS)], loc_sem.at[1]),
        pltpu.make_async_copy(wu_ref.at[0], wu.at[:, pl.ds(0, hid_n)], loc_sem.at[2]),
        pltpu.make_async_copy(wd_ref.at[0], wd.at[:, pl.ds(0, hid_n)], loc_sem.at[3]),
    ]
    for copy in own:
        copy.start()
    names = lax.broadcasted_iota(jnp.int32, (EXP, ROWS), 0)
    dense = jnp.zeros((EXP, ROWS), F32)
    for k in range(ids_ref.shape[0]):
        dense = dense + jnp.where(ids_ref[k : k + 1, :] == names, gates_ref[k : k + 1, :].astype(F32), 0.0)
    gt[NZ - 2] = dense.astype(BF16)
    pl.semaphore_wait(barrier, len(partners))

    def remote(src, dst, ssem, rsem, device):
        return pltpu.make_async_remote_copy(
            src_ref=src, dst_ref=dst, send_sem=ssem, recv_sem=rsem,
            device_id=device, device_id_type=MESH,
        )

    bufs = (xb, db)
    last_way = (0, 1, 0)

    def block(arr, k):
        if arr == 2:
            return gt.at[k]
        return bufs[arr].at[pl.ds(k * ROWS, ROWS)]

    def slot(s, r):
        return NZ - 1 if s == 4 else 2 * (s - 1) + r

    sent = []

    def send_block(arr, r, s, src):
        copy = remote(src, block(arr, slot(s, r)), ag_send.at[arr, r, s - 1], ag_recv.at[arr, r, s], zdev[r])
        copy.start()
        sent.append(copy)

    def arrive(arr, s):
        for r in range(2):
            if s == 4 and last_way[arr] != r:
                continue
            here = block(arr, slot(s, r))
            remote(here, here, ag_send.at[arr, r, 0], ag_recv.at[arr, r, s], zdev[r]).wait_recv()
            if s < 3 or (s == 3 and last_way[arr] == r):
                send_block(arr, r, s + 1, here)

    for arr, src in ((0, x_ref), (1, dy_ref), (2, gt.at[NZ - 2])):
        for r in range(2):
            send_block(arr, r, 1, src)
    part = width // 2
    weight_first, weight_core, weight_relay = [], [], []
    for h in range(2):
        for m, (src, buf, far) in enumerate(((wu_ref, wu, y_pair), (wd_ref, wd, y_other))):
            rows = pl.ds(h * part, part)
            lanes = [pl.ds(j * hid_n, hid_n) for j in range(4)]
            weight_first.append(remote(
                src.at[0, rows], buf.at[rows, lanes[1]], w_send.at[m, h, 0], w_recv.at[m, h, 0], far))
            weight_core.append(remote(
                src.at[0, rows], buf.at[rows, lanes[2]], w_send.at[m, h, 1], w_recv.at[m, h, 1], cdev))
            weight_relay.append(remote(
                buf.at[rows, lanes[1]], buf.at[rows, lanes[3]], w_send.at[m, h, 2], w_recv.at[m, h, 2], cdev))
    for copy in weight_first + weight_core:
        copy.start()

    lane = lax.broadcasted_iota(jnp.int32, (1, LANES), 1)
    lane32 = lax.broadcasted_iota(jnp.int32, (1, EXP), 1)
    chunk = 32
    slots = [((yl if j % 2 == 0 else 1 - yl) * NZ + z) * 2 + (core if j < 2 else 1 - core) for j in range(4)]

    def compute(k, blocks):
        base, size = k * ROWS, blocks * ROWS
        rows = pl.ds(base, size)
        for b in range(blocks):
            gs[pl.ds(b * ROWS, ROWS), :] = gt[k + b].astype(F32).T

        def hidden_part(n, carry):
            at = pl.ds(pl.multiple_of(n * 512, 512), 512)
            pre_s[:size, at] = jnp.dot(xb[rows, :], wu[:, at], preferred_element_type=F32)
            bh_s[:size, at] = jnp.dot(db[rows, :], wd[:, at], preferred_element_type=F32)
            return carry

        lax.fori_loop(0, 4 * hid_n // 512, hidden_part, 0)

        def piece(q, carry):
            at = pl.multiple_of(q * chunk, chunk)
            sub = pl.ds(at, chunk)
            big = pl.ds(pl.multiple_of(base + at, chunk), chunk)
            out = jnp.zeros((chunk, LANES), F32)
            for j in range(4):
                lanes = pl.ds(j * hid_n, hid_n)
                g = jnp.sum(jnp.where(lane32 == slots[j], gs[sub, :], 0.0), axis=1, keepdims=True)
                pre, bh = pre_s[sub, lanes], bh_s[sub, lanes]
                sig = 0.5 * jnp.tanh(0.5 * pre) + 0.5
                hidden = (pre * sig).astype(BF16).astype(F32)
                gate = jnp.sum(bh * hidden, axis=1, keepdims=True)
                slope = sig * (1.0 + pre * (1.0 - sig))
                gp[sub, lanes] = (g * bh * slope).astype(BF16)
                gh[big, lanes] = (g * hidden).astype(BF16)
                out = jnp.where(lane == slots[j], gate, out)
            gq[sub, :] = out
            return carry

        lax.fori_loop(0, size // chunk, piece, 0)
        for b in range(blocks):
            pg[k + b] = gq[pl.ds(b * ROWS, ROWS), :].T[:EXP, :].astype(BF16)

        def columns(t, carry):
            at = pl.ds(pl.multiple_of(t * 512, 512), 512)
            pb[rows, at] = lax.dot_general(
                gp[:size, :], wu[at, :], (((1,), (1,)), ((), ())), preferred_element_type=F32).astype(BF16)
            return carry

        lax.fori_loop(0, width // 512, columns, 0)

    deep = NZ * ROWS // 2

    def down_tile(phase):
        def body(q, carry):
            d = jnp.where(q == 0, 2, jnp.where(q == 3, 0, jnp.where(q == 2, 3, 1)))
            at = pl.ds(pl.multiple_of(lax.rem(x + d, NX) * tile, tile), tile)
            for k in range(deep // ROWS):
                dyt[:, pl.ds(k * ROWS, ROWS)] = db[pl.ds(phase * deep + k * ROWS, ROWS), at].T
            rows = pl.ds(phase * deep, deep)
            for dst, start in ((s_s, 2 * hid_n), (a_s, 0)):
                term = jnp.dot(dyt[...], gh[rows, pl.ds(start, 2 * hid_n)], preferred_element_type=F32)
                if phase:
                    term = term + dst[q].astype(F32)
                dst[q] = term.astype(BF16)
            if phase:
                remote(s_s.at[q], r_s.at[q], c_send.at[q], c_recv.at[q], cdev).start()
            return carry
        return body

    cols = (pl.ds(0, HALF), pl.ds(HALF, width - HALF))
    back = (zdev[1], zdev[0])

    def rs_copy(r, t, h):
        k = slot(4 - t, r)
        if h == 2:
            src, dst = pg.at[k], rg.at[r, t]
        else:
            src, dst = pb.at[pl.ds(k * ROWS, ROWS), cols[h]], rb.at[r, t, :, cols[h]]
        return remote(src, dst, rs_send.at[r, t, h], rs_recv.at[r, t, h], back[r])

    def rs_add(r, t, h):
        rs_copy(r, t - 1, h).wait_recv()
        k = slot(4 - t, r)
        if h == 2:
            pg[k] = (pg[k].astype(F32) + rg[r, t - 1].astype(F32)).astype(BF16)
        else:
            row = pl.ds(k * ROWS, ROWS)
            pb[row, cols[h]] = (
                pb[row, cols[h]].astype(F32) + rb[r, t - 1, :, cols[h]].astype(F32)).astype(BF16)
        rs_copy(r, t, h).start()

    def rs_free(t):
        for r in range(2):
            rs_add(r, t, 1 - r)

    def rs_tied(t):
        for r in range(2):
            rs_add(r, t, r)
        for r in range(2):
            if t > 1 or r == 0:
                rs_add(r, t, 2)

    for arr in (0, 1, 2):
        arrive(arr, 1)
    for first, relay in zip(weight_first, weight_relay):
        first.wait_recv()
        relay.start()
    for copy in own:
        copy.wait()
    for copy in weight_core + weight_relay:
        copy.wait_recv()
    compute(NZ - 2, 1)
    arrive(0, 2)
    compute(0, 2)
    arrive(1, 2)
    arrive(2, 2)
    compute(2, 2)
    arrive(0, 3)
    lax.fori_loop(0, NX, down_tile(0), 0)
    arrive(1, 3)
    arrive(2, 3)
    compute(4, 2)
    for r in range(2):
        rs_copy(r, 1, 1 - r).start()
    rs_copy(1, 1, 2).start()
    for arr in (0, 1, 2):
        arrive(arr, 4)
    compute(NZ - 1, 1)
    for r in range(2):
        rs_copy(r, 0, r).start()
    rs_copy(0, 0, 2).start()
    rs_free(2)
    lax.fori_loop(0, 2, down_tile(1), 0)
    rs_tied(1)
    lax.fori_loop(2, NX, down_tile(1), 0)
    rs_free(3)

    def core_copy(q):
        return remote(s_s.at[q], r_s.at[q], c_send.at[q], c_recv.at[q], cdev)

    def add_into(dst, *others):
        total = dst[...].astype(F32)
        for other in others:
            total = total + other[...].astype(F32)
        dst[...] = total.astype(BF16)

    def half(jj):
        return pl.ds(jj * hid_n, hid_n)

    def x_first(r):
        return remote(a_s.at[0, :, half(r)], x1.at[r], x_send.at[0, r, 0], x_recv.at[0, r, 0], xdev[r])

    def x_second(r, jj):
        return remote(
            a_s.at[1 + r, :, half(jj)], x2.at[r, jj], x_send.at[1, r, jj], x_recv.at[1, r, jj], xdev[r])

    core_copy(0).wait_recv()
    add_into(a_s.at[0], r_s.at[0])
    for r in range(2):
        x_first(r).start()
    for r in range(2):
        core_copy(1 + r).wait_recv()
        add_into(a_s.at[1 + r], r_s.at[1 + r])
        x_second(r, 1 - r).start()
    core_copy(3).wait_recv()
    add_into(a_s.at[3], r_s.at[3])
    rs_tied(2)
    for r in range(2):
        x_first(r).wait_recv()
        add_into(a_s.at[1 + r, :, half(r)], x1.at[r])
        x_second(r, r).start()
    rs_tied(3)

    def y_copy(d):
        row = pl.multiple_of((lax.rem(yy + d, NY) // 2) * ROWS, ROWS)
        return remote(
            a_s.at[3, pl.ds(row, ROWS), half(d % 2)], yr.at[d - 1], y_send.at[d - 1], y_recv.at[d - 1], ydev[d])

    for r in range(2):
        x_second(r, 1 - r).wait_recv()
    for r in range(2):
        x_second(r, r).wait_recv()
    for jj in range(2):
        add_into(a_s.at[3, :, half(jj)], x2.at[0, jj], x2.at[1, jj])
        for d in ((4, 2, 6) if jj == 0 else (3, 5, 1, 7)):
            y_copy(d).start()

    mine = pl.ds(OWN, ROWS)
    for h in (1, 0):
        for r in range(2):
            rs_copy(r, 3, r ^ h).wait_recv()
    for h in range(2):
        tok_ref[:, cols[h]] = (
            pb[mine, cols[h]].astype(F32) + rb[0, 3, :, cols[h]].astype(F32) + rb[1, 3, :, cols[h]].astype(F32)
        ).astype(BF16)
    for r in range(2):
        rs_copy(r, 3, 2).wait_recv()
    gates = pg[NZ - 2].astype(F32) + rg[0, 3].astype(F32) + rg[1, 3].astype(F32)
    for k in range(ids_ref.shape[0]):
        picked = jnp.where(ids_ref[k : k + 1, :] == names, gates, 0.0)
        gg_ref[k : k + 1, :] = jnp.sum(picked, axis=0, keepdims=True)

    total = a_s[3, pl.ds(pl.multiple_of(yh * ROWS, ROWS), ROWS), half(0)].astype(F32)
    for d in range(1, NY):
        y_copy(d).wait_recv()
        total = total + yr[d - 1].astype(F32)
    dg_ref[...] = total

    for copy in sent + weight_first + weight_core + weight_relay:
        copy.wait_send()
    for r in range(2):
        for t in range(4):
            for h in range(3):
                if t == 0 and h != (r if h < 2 else 2 + r):
                    continue
                rs_copy(r, t, h).wait_send()
        x_first(r).wait_send()
        for jj in range(2):
            x_second(r, jj).wait_send()
    for q in range(NX):
        core_copy(q).wait_send()
    for d in range(1, NY):
        y_copy(d).wait_send()


def shards(tokens, cotangent, expert_ids, gate_weights, w_up, w_down):
    rows, width = tokens.shape
    hid_n = w_up.shape[2]
    tile = width // NX
    dma, vmem = pltpu.SemaphoreType.DMA, pltpu.VMEM
    hbm = pl.BlockSpec(memory_space=pl.ANY)
    local = pl.BlockSpec(memory_space=pltpu.VMEM)
    token_grad, gates, down = pl.pallas_call(
        kernel,
        out_shape=(
            jax.ShapeDtypeStruct((rows, width), BF16),
            jax.ShapeDtypeStruct((expert_ids.shape[1], rows), F32),
            jax.ShapeDtypeStruct((width // (NX * NYH), hid_n), F32),
        ),
        in_specs=[hbm] * 4 + [local] * 2,
        out_specs=[local] * 3,
        scratch_shapes=[
            vmem((NZ * rows, width), BF16),
            vmem((NZ * rows, width), BF16),
            vmem((NZ, EXP, rows), BF16),
            vmem((width, 4 * hid_n), BF16),
            vmem((width, 4 * hid_n), BF16),
            vmem((NZ * rows, 4 * hid_n), BF16),
            vmem((2 * rows, 4 * hid_n), BF16),
            vmem((2 * rows, 4 * hid_n), F32),
            vmem((2 * rows, 4 * hid_n), F32),
            vmem((2 * rows, EXP), F32),
            vmem((2 * rows, LANES), F32),
            vmem((NZ * rows, width), BF16),
            vmem((NZ, EXP, rows), BF16),
            vmem((2, 4, rows, width), BF16),
            vmem((2, 4, EXP, rows), BF16),
            vmem((tile, NZ * rows // 2), BF16),
            vmem((NX, tile, 2 * hid_n), BF16),
            vmem((NX, tile, 2 * hid_n), BF16),
            vmem((NX, tile, 2 * hid_n), BF16),
            vmem((2, tile, hid_n), BF16),
            vmem((2, 2, tile, hid_n), BF16),
            vmem((NY - 1, rows, hid_n), BF16),
            dma((4,)),
            dma((3, 2, 4)),
            dma((3, 2, 5)),
            dma((2, 2, 3)),
            dma((2, 2, 3)),
            dma((2, 4, 3)),
            dma((2, 4, 3)),
            dma((NX,)),
            dma((NX,)),
            dma((2, 2, 2)),
            dma((2, 2, 2)),
            dma((NY - 1,)),
            dma((NY - 1,)),
        ],
        compiler_params=pltpu.CompilerParams(
            collective_id=0, has_side_effects=True, vmem_limit_bytes=66_000_000
        ),
        name="expert_backward",
    )(tokens, cotangent, w_up, w_down, expert_ids.T, gate_weights.T)
    return token_grad, gates.T.astype(BF16), down[None]


def solution(mesh):
    return jax.shard_map(
        shards,
        mesh=mesh,
        in_specs=(
            P(("dp", "ep"), None),
            P(("dp", "ep"), None),
            P(("dp", "ep"), None),
            P(("dp", "ep"), None),
            P("ep", None, None),
            P("ep", None, None),
        ),
        out_specs=(P(("dp", "ep"), None), P(("dp", "ep"), None), P("ep", "dp", None)),
        check_vma=False,
    )
```

```python
import jax
import jax.numpy as jnp
from jax import lax
from jax.experimental import pallas as pl
from jax.experimental.pallas import tpu as pltpu
from jax.sharding import PartitionSpec as P

MESH = pl.DeviceIdType.MESH
BF16, F32 = jnp.bfloat16, jnp.float32
NX, NYH, NZ = 4, 4, 8
NY = 2 * NYH
ROWS = 128
LANES = 128
HALF = 1024
EXP = 32
MID = 64


def kernel(
    x_ref, dy_ref, wu_ref, wd_ref, ids_ref, gates_ref, tok_ref, gg_ref, dg_ref,
    xb, db, gt, wu, wd, gh, gp, pre_s, bh_s, gs, gq, pb, pg, rb, rg, dyt, a1, a2, s1, s2, r1, r2, rx1, ry1, ry2, rx2,
    loc_sem, ag_send, ag_recv, w_send, w_recv, rs_send, rs_recv, c_send, c_recv, x_sems, y1_sems, y2_sems, x2_sems,
):
    width = dy_ref.shape[1]
    hid_n = wu_ref.shape[2]
    tile = width // NX
    dp, ep = lax.axis_index("dp"), lax.axis_index("ep")
    core = lax.rem(ep, 2)
    z = lax.rem(ep // 2, NZ)
    yl = ep // (2 * NZ)
    x, yh = dp // NYH, lax.rem(dp, NYH)
    yy = 2 * yh + yl

    def dev(x_, y_, z_, c_):
        return (x_ * NYH + y_ // 2, (lax.rem(y_, 2) * NZ + z_) * 2 + c_)

    zdev = [dev(x, yy, lax.rem(z + 1, NZ), core), dev(x, yy, lax.rem(z + NZ - 1, NZ), core)]
    cdev = dev(x, yy, z, 1 - core)
    ydev = [dev(x, lax.rem(yy + 1, NY), z, core), dev(x, lax.rem(yy + NY - 1, NY), z, core)]
    y_pair = dev(x, lax.rem(yy + NY + 1 - 2 * yl, NY), z, core)
    y_other = dev(x, lax.rem(yy + NY + 2 * yl - 1, NY), z, core)
    xdev = [dev(lax.rem(x + 1, NX), yy, z, core), dev(lax.rem(x + NX - 1, NX), yy, z, core)]

    barrier = pltpu.get_barrier_semaphore()
    partners = zdev + [cdev] + ydev + xdev
    for device in partners:
        pl.semaphore_signal(barrier, inc=1, device_id=device, device_id_type=MESH)

    OWN, FAR = (NZ - 2) * ROWS, (NZ - 1) * ROWS
    own = [
        pltpu.make_async_copy(x_ref, xb.at[pl.ds(OWN, ROWS)], loc_sem.at[0]),
        pltpu.make_async_copy(dy_ref, db.at[pl.ds(OWN, ROWS)], loc_sem.at[1]),
        pltpu.make_async_copy(wu_ref.at[0], wu.at[:, pl.ds(0, hid_n)], loc_sem.at[2]),
        pltpu.make_async_copy(wd_ref.at[0], wd.at[:, pl.ds(0, hid_n)], loc_sem.at[3]),
    ]
    for copy in own:
        copy.start()
    names = lax.broadcasted_iota(jnp.int32, (EXP, ROWS), 0)
    dense = jnp.zeros((EXP, ROWS), F32)
    for k in range(ids_ref.shape[0]):
        dense = dense + jnp.where(ids_ref[k : k + 1, :] == names, gates_ref[k : k + 1, :].astype(F32), 0.0)
    gt[NZ - 2] = dense.astype(BF16)
    pl.semaphore_wait(barrier, len(partners))

    def remote(src, dst, ssem, rsem, device):
        return pltpu.make_async_remote_copy(
            src_ref=src, dst_ref=dst, send_sem=ssem, recv_sem=rsem,
            device_id=device, device_id_type=MESH,
        )

    bufs = (xb, db)
    last_way = (0, 1, 0)

    def block(arr, k):
        if arr == 2:
            return gt.at[k]
        return bufs[arr].at[pl.ds(k * ROWS, ROWS)]

    def slot(s, r):
        return NZ - 1 if s == 4 else 2 * (s - 1) + r

    sent = []

    def send_block(arr, r, s, src):
        copy = remote(src, block(arr, slot(s, r)), ag_send.at[arr, r, s - 1], ag_recv.at[arr, r, s], zdev[r])
        copy.start()
        sent.append(copy)

    def arrive(arr, s):
        for r in range(2):
            if s == 4 and last_way[arr] != r:
                continue
            here = block(arr, slot(s, r))
            remote(here, here, ag_send.at[arr, r, 0], ag_recv.at[arr, r, s], zdev[r]).wait_recv()
            if s < 3 or (s == 3 and last_way[arr] == r):
                send_block(arr, r, s + 1, here)

    for arr, src in ((0, x_ref), (1, dy_ref), (2, gt.at[NZ - 2])):
        for r in range(2):
            send_block(arr, r, 1, src)
    part = width // 2
    weight_first, weight_core, weight_relay = [], [], []
    for h in range(2):
        for m, (src, buf, far) in enumerate(((wu_ref, wu, y_pair), (wd_ref, wd, y_other))):
            rows = pl.ds(h * part, part)
            lanes = [pl.ds(j * hid_n, hid_n) for j in range(4)]
            weight_first.append(remote(
                src.at[0, rows], buf.at[rows, lanes[1]], w_send.at[m, h, 0], w_recv.at[m, h, 0], far))
            weight_core.append(remote(
                src.at[0, rows], buf.at[rows, lanes[2]], w_send.at[m, h, 1], w_recv.at[m, h, 1], cdev))
            weight_relay.append(remote(
                buf.at[rows, lanes[1]], buf.at[rows, lanes[3]], w_send.at[m, h, 2], w_recv.at[m, h, 2], cdev))
    for copy in weight_first + weight_core:
        copy.start()

    lane = lax.broadcasted_iota(jnp.int32, (1, LANES), 1)
    lane32 = lax.broadcasted_iota(jnp.int32, (1, EXP), 1)
    chunk = 32
    slots = [((yl if j % 2 == 0 else 1 - yl) * NZ + z) * 2 + (core if j < 2 else 1 - core) for j in range(4)]

    def compute(k, blocks):
        base, size = k * ROWS, blocks * ROWS
        rows = pl.ds(base, size)
        for b in range(blocks):
            gs[pl.ds(b * ROWS, ROWS), :] = gt[k + b].astype(F32).T

        def hidden_part(n, carry):
            at = pl.ds(pl.multiple_of(n * 512, 512), 512)
            pre_s[:size, at] = jnp.dot(xb[rows, :], wu[:, at], preferred_element_type=F32)
            bh_s[:size, at] = jnp.dot(db[rows, :], wd[:, at], preferred_element_type=F32)
            return carry

        lax.fori_loop(0, 4 * hid_n // 512, hidden_part, 0)

        def piece(q, carry):
            at = pl.multiple_of(q * chunk, chunk)
            sub = pl.ds(at, chunk)
            big = pl.ds(pl.multiple_of(base + at, chunk), chunk)
            out = jnp.zeros((chunk, LANES), F32)
            for j in range(4):
                lanes = pl.ds(j * hid_n, hid_n)
                g = jnp.sum(jnp.where(lane32 == slots[j], gs[sub, :], 0.0), axis=1, keepdims=True)
                pre, bh = pre_s[sub, lanes], bh_s[sub, lanes]
                sig = 0.5 * jnp.tanh(0.5 * pre) + 0.5
                hidden = (pre * sig).astype(BF16).astype(F32)
                gate = jnp.sum(bh * hidden, axis=1, keepdims=True)
                slope = sig * (1.0 + pre * (1.0 - sig))
                gp[sub, lanes] = (g * bh * slope).astype(BF16)
                gh[big, lanes] = (g * hidden).astype(BF16)
                out = jnp.where(lane == slots[j], gate, out)
            gq[sub, :] = out
            return carry

        lax.fori_loop(0, size // chunk, piece, 0)
        for b in range(blocks):
            pg[k + b] = gq[pl.ds(b * ROWS, ROWS), :].T[:EXP, :].astype(BF16)

        def columns(t, carry):
            at = pl.ds(pl.multiple_of(t * 512, 512), 512)
            pb[rows, at] = lax.dot_general(
                gp[:size, :], wu[at, :], (((1,), (1,)), ((), ())), preferred_element_type=F32).astype(BF16)
            return carry

        lax.fori_loop(0, width // 512, columns, 0)

    def core_copy(q, part):
        src, dst = ((s1.at[q], r1.at[q]), (s2.at[:, q], r2.at[:, q]))[part]
        return remote(src, dst, c_send.at[q, part], c_recv.at[q, part], cdev)

    deep = NZ * ROWS // 2

    def down_tile(phase):
        def body(q, carry):
            d = jnp.where(q == 0, 2, jnp.where(q == 3, 0, jnp.where(q == 2, 3, 1)))
            at = pl.ds(pl.multiple_of(lax.rem(x + d, NX) * tile, tile), tile)
            for k in range(deep // ROWS):
                dyt[:, pl.ds(k * ROWS, ROWS)] = db[pl.ds(phase * deep + k * ROWS, ROWS), at].T
            rows = pl.ds(phase * deep, deep)
            for by_x, by_y, start in ((s1, s2, 2 * hid_n), (a1, a2, 0)):
                term = jnp.dot(dyt[...], gh[rows, pl.ds(start, 2 * hid_n)], preferred_element_type=F32)
                for jj in range(2):
                    for row in range(NYH):
                        top = row * ROWS
                        upper = term[top : top + MID, jj * hid_n : (jj + 1) * hid_n]
                        lower = term[top + MID : top + ROWS, jj * hid_n : (jj + 1) * hid_n]
                        k = lax.rem(2 * row + (yl if jj == 0 else 1 - yl) + NY - yy, NY)
                        if phase:
                            upper = upper + by_x[q, jj, row].astype(F32)
                            lower = lower + by_y[k, q].astype(F32)
                        by_x[q, jj, row] = upper.astype(BF16)
                        by_y[k, q] = lower.astype(BF16)
            if phase:
                for half in range(2):
                    core_copy(q, half).start()
            return carry
        return body

    cols = (pl.ds(0, HALF), pl.ds(HALF, width - HALF))
    back = (zdev[1], zdev[0])

    def rs_copy(r, t, h):
        k = slot(4 - t, r)
        if h == 2:
            src, dst = pg.at[k], rg.at[r, t]
        else:
            src, dst = pb.at[pl.ds(k * ROWS, ROWS), cols[h]], rb.at[r, t, :, cols[h]]
        return remote(src, dst, rs_send.at[r, t, h], rs_recv.at[r, t, h], back[r])

    def rs_add(r, t, h):
        rs_copy(r, t - 1, h).wait_recv()
        k = slot(4 - t, r)
        if h == 2:
            pg[k] = (pg[k].astype(F32) + rg[r, t - 1].astype(F32)).astype(BF16)
        else:
            row = pl.ds(k * ROWS, ROWS)
            pb[row, cols[h]] = (
                pb[row, cols[h]].astype(F32) + rb[r, t - 1, :, cols[h]].astype(F32)).astype(BF16)
        rs_copy(r, t, h).start()

    def rs_free(t):
        for r in range(2):
            rs_add(r, t, 1 - r)

    def rs_tied(t):
        for r in range(2):
            rs_add(r, t, r)
        for r in range(2):
            if t > 1 or r == 0:
                rs_add(r, t, 2)

    for arr in (0, 1, 2):
        arrive(arr, 1)
    for first, relay in zip(weight_first, weight_relay):
        first.wait_recv()
        relay.start()
    for copy in own:
        copy.wait()
    for copy in weight_core + weight_relay:
        copy.wait_recv()
    compute(NZ - 2, 1)
    arrive(0, 2)
    compute(0, 2)
    arrive(1, 2)
    arrive(2, 2)
    compute(2, 2)
    arrive(0, 3)
    lax.fori_loop(0, NX, down_tile(0), 0)
    arrive(1, 3)
    arrive(2, 3)
    compute(4, 2)
    for r in range(2):
        rs_copy(r, 1, 1 - r).start()
    rs_copy(1, 1, 2).start()
    for arr in (0, 1, 2):
        arrive(arr, 4)
    compute(NZ - 1, 1)
    for r in range(2):
        rs_copy(r, 0, r).start()
    rs_copy(0, 0, 2).start()
    rs_free(2)
    lax.fori_loop(0, 2, down_tile(1), 0)
    rs_tied(1)
    lax.fori_loop(2, NX, down_tile(1), 0)
    rs_free(3)

    def add_into(dst, *others):
        total = dst[...].astype(F32)
        for other in others:
            total = total + other[...].astype(F32)
        dst[...] = total.astype(BF16)

    class Ring:
        def __init__(self, n, piece, recv, sems, devices):
            self.n, self.piece, self.recv, self.sems, self.devices = n, piece, recv, sems, devices
            self.started = []

        def copy(self, r, t, h):
            m = self.n // 2 - t
            return remote(
                self.piece(m if r == 0 else self.n - m, h), self.recv.at[r, t, h],
                self.sems.at[0, r, t, h], self.sems.at[1, r, t, h], self.devices[r])

        def send(self, r, t, h):
            self.copy(r, t, h).start()
            self.started.append((r, t, h))

        def begin(self):
            for r in range(2):
                self.send(r, 0, r)

        def forward(self, t, free):
            for r in range(2):
                h = 1 - r if free else r
                if t > 1 or not free:
                    m = self.n // 2 - t
                    self.copy(r, t - 1, h).wait_recv()
                    add_into(self.piece(m if r == 0 else self.n - m, h), self.recv.at[r, t - 1, h])
                self.send(r, t, h)

        def finish(self):
            t = self.n // 2 - 1
            for free in (1, 0):
                for r in range(2):
                    self.copy(r, t, 1 - r if free else r).wait_recv()
            for h in range(2):
                add_into(self.piece(0, h), self.recv.at[0, t, h], self.recv.at[1, t, h])

        def drain(self):
            for r, t, h in self.started:
                self.copy(r, t, h).wait_send()

    place = {2: 0, 1: 1, NX - 1: 2, 0: 3}
    sub = MID // 2

    def y_row(k):
        return lax.rem(yy + k, NY) // 2

    ring_x1 = Ring(NX, lambda k, h: a1.at[place[k], h], rx1, x_sems, xdev)
    ring_y1 = Ring(NY, lambda k, h: a1.at[3, k % 2, y_row(k), pl.ds(h * sub, sub)], ry1, y1_sems, ydev)
    ring_y2 = Ring(NY, lambda k, h: a2.at[k, pl.ds(2 * h, 2)], ry2, y2_sems, ydev)
    ring_x2 = Ring(NX, lambda k, h: a2.at[0, place[k], pl.ds(h * sub, sub)], rx2, x2_sems, xdev)

    for q in range(3):
        core_copy(q, 0).wait_recv()
        for jj in range(2):
            add_into(a1.at[q, jj], r1.at[q, jj])
        if q == 0:
            ring_x1.begin()
    ring_x1.forward(1, True)
    for q in range(NX):
        core_copy(q, 1).wait_recv()
    for k in (NY // 2, 3, 5):
        add_into(a2.at[k], r2.at[k])
        if k == NY // 2:
            ring_y2.begin()
    ring_y2.forward(1, True)
    for k in (2, 6, 1, 7, 0):
        add_into(a2.at[k], r2.at[k])
    core_copy(3, 0).wait_recv()
    for jj in range(2):
        add_into(a1.at[3, jj], r1.at[3, jj])
    ring_x1.forward(1, False)
    ring_y2.forward(2, True)
    ring_y2.forward(1, False)
    rs_tied(2)
    ring_y2.forward(3, True)
    ring_y2.forward(2, False)
    ring_x1.finish()
    ring_y1.begin()
    ring_y1.forward(1, True)
    ring_y2.forward(3, False)
    rs_tied(3)
    ring_y1.forward(2, True)
    ring_y1.forward(1, False)
    ring_y2.finish()
    ring_x2.begin()
    ring_x2.forward(1, True)
    ring_y1.forward(3, True)
    ring_y1.forward(2, False)
    ring_x2.forward(1, False)
    ring_y1.forward(3, False)

    mine = pl.ds(OWN, ROWS)
    for h in (1, 0):
        for r in range(2):
            rs_copy(r, 3, r ^ h).wait_recv()
    for h in range(2):
        tok_ref[:, cols[h]] = (
            pb[mine, cols[h]].astype(F32) + rb[0, 3, :, cols[h]].astype(F32) + rb[1, 3, :, cols[h]].astype(F32)
        ).astype(BF16)
    for r in range(2):
        rs_copy(r, 3, 2).wait_recv()
    gates = pg[NZ - 2].astype(F32) + rg[0, 3].astype(F32) + rg[1, 3].astype(F32)
    for k in range(ids_ref.shape[0]):
        picked = jnp.where(ids_ref[k : k + 1, :] == names, gates, 0.0)
        gg_ref[k : k + 1, :] = jnp.sum(picked, axis=0, keepdims=True)

    ring_x2.finish()
    dg_ref[MID:, :] = a2[0, 3].astype(F32)
    ring_y1.finish()
    dg_ref[:MID, :] = a1[3, 0, yh].astype(F32)

    for copy in sent + weight_first + weight_core + weight_relay:
        copy.wait_send()
    for r in range(2):
        for t in range(4):
            for h in range(3):
                if t == 0 and h != (r if h < 2 else 2 + r):
                    continue
                rs_copy(r, t, h).wait_send()
    for q in range(NX):
        for half in range(2):
            core_copy(q, half).wait_send()
    for ring in (ring_x1, ring_y1, ring_y2, ring_x2):
        ring.drain()


def shards(tokens, cotangent, expert_ids, gate_weights, w_up, w_down):
    rows, width = tokens.shape
    hid_n = w_up.shape[2]
    tile = width // NX
    dma, vmem = pltpu.SemaphoreType.DMA, pltpu.VMEM
    hbm = pl.BlockSpec(memory_space=pl.ANY)
    local = pl.BlockSpec(memory_space=pltpu.VMEM)
    token_grad, gates, down = pl.pallas_call(
        kernel,
        out_shape=(
            jax.ShapeDtypeStruct((rows, width), BF16),
            jax.ShapeDtypeStruct((expert_ids.shape[1], rows), F32),
            jax.ShapeDtypeStruct((width // (NX * NYH), hid_n), F32),
        ),
        in_specs=[hbm] * 4 + [local] * 2,
        out_specs=[local] * 3,
        scratch_shapes=[
            vmem((NZ * rows, width), BF16),
            vmem((NZ * rows, width), BF16),
            vmem((NZ, EXP, rows), BF16),
            vmem((width, 4 * hid_n), BF16),
            vmem((width, 4 * hid_n), BF16),
            vmem((NZ * rows, 4 * hid_n), BF16),
            vmem((2 * rows, 4 * hid_n), BF16),
            vmem((2 * rows, 4 * hid_n), F32),
            vmem((2 * rows, 4 * hid_n), F32),
            vmem((2 * rows, EXP), F32),
            vmem((2 * rows, LANES), F32),
            vmem((NZ * rows, width), BF16),
            vmem((NZ, EXP, rows), BF16),
            vmem((2, 4, rows, width), BF16),
            vmem((2, 4, EXP, rows), BF16),
            vmem((tile, NZ * rows // 2), BF16),
            vmem((NX, 2, NYH, MID, hid_n), BF16),
            vmem((NY, NX, MID, hid_n), BF16),
            vmem((NX, 2, NYH, MID, hid_n), BF16),
            vmem((NY, NX, MID, hid_n), BF16),
            vmem((NX, 2, NYH, MID, hid_n), BF16),
            vmem((NY, NX, MID, hid_n), BF16),
            vmem((2, 2, 2, NYH, MID, hid_n), BF16),
            vmem((2, 4, 2, MID // 2, hid_n), BF16),
            vmem((2, 4, 2, 2, MID, hid_n), BF16),
            vmem((2, 2, 2, MID // 2, hid_n), BF16),
            dma((4,)),
            dma((3, 2, 4)),
            dma((3, 2, 5)),
            dma((2, 2, 3)),
            dma((2, 2, 3)),
            dma((2, 4, 3)),
            dma((2, 4, 3)),
            dma((NX, 2)),
            dma((NX, 2)),
            dma((2, 2, 2, 2)),
            dma((2, 2, 4, 2)),
            dma((2, 2, 4, 2)),
            dma((2, 2, 2, 2)),
        ],
        compiler_params=pltpu.CompilerParams(
            collective_id=0, has_side_effects=True, vmem_limit_bytes=66_000_000
        ),
        name="expert_backward",
    )(tokens, cotangent, w_up, w_down, expert_ids.T, gate_weights.T)
    return token_grad, gates.T.astype(BF16), down[None]


def solution(mesh):
    return jax.shard_map(
        shards,
        mesh=mesh,
        in_specs=(
            P(("dp", "ep"), None),
            P(("dp", "ep"), None),
            P(("dp", "ep"), None),
            P(("dp", "ep"), None),
            P("ep", None, None),
            P("ep", None, None),
        ),
        out_specs=(P(("dp", "ep"), None), P(("dp", "ep"), None), P("ep", "dp", None)),
        check_vma=False,
    )
```

```python
import jax
import jax.numpy as jnp
from jax import lax
from jax.experimental import pallas as pl
from jax.experimental.pallas import tpu as pltpu
from jax.sharding import PartitionSpec as P

MESH = pl.DeviceIdType.MESH
BF16, F32 = jnp.bfloat16, jnp.float32
NX, NYH, NZ = 4, 4, 8
NY = 2 * NYH
ROWS = 128
LANES = 128
HALF = 1024
EXP = 32
MID = 64


def kernel(
    x_ref, dy_ref, wu_ref, wd_ref, ids_ref, gates_ref, tok_ref, gg_ref, dg_ref,
    xb, db, gt, wu, wd, gh, gp, pre_s, bh_s, gs, gq, pb, pg, rb, rg, dyt, a1, a2, s1, s2, r1, r2, rx1, ry1, ry2, rx2,
    loc_sem, ag_send, ag_recv, w_send, w_recv, rs_send, rs_recv, c_send, c_recv, x_sems, y1_sems, y2_sems, x2_sems,
):
    width = dy_ref.shape[1]
    hid_n = wu_ref.shape[2]
    tile = width // NX
    dp, ep = lax.axis_index("dp"), lax.axis_index("ep")
    core = lax.rem(ep, 2)
    z = lax.rem(ep // 2, NZ)
    yl = ep // (2 * NZ)
    x, yh = dp // NYH, lax.rem(dp, NYH)
    yy = 2 * yh + yl

    def dev(x_, y_, z_, c_):
        return (x_ * NYH + y_ // 2, (lax.rem(y_, 2) * NZ + z_) * 2 + c_)

    zdev = [dev(x, yy, lax.rem(z + 1, NZ), core), dev(x, yy, lax.rem(z + NZ - 1, NZ), core)]
    cdev = dev(x, yy, z, 1 - core)
    ydev = [dev(x, lax.rem(yy + 1, NY), z, core), dev(x, lax.rem(yy + NY - 1, NY), z, core)]
    y_pair = dev(x, lax.rem(yy + NY + 1 - 2 * yl, NY), z, core)
    y_other = dev(x, lax.rem(yy + NY + 2 * yl - 1, NY), z, core)
    xdev = [dev(lax.rem(x + 1, NX), yy, z, core), dev(lax.rem(x + NX - 1, NX), yy, z, core)]

    barrier = pltpu.get_barrier_semaphore()
    partners = zdev + [cdev] + ydev + xdev
    for device in partners:
        pl.semaphore_signal(barrier, inc=1, device_id=device, device_id_type=MESH)

    OWN, FAR = (NZ - 2) * ROWS, (NZ - 1) * ROWS
    own = [
        pltpu.make_async_copy(x_ref, xb.at[pl.ds(OWN, ROWS)], loc_sem.at[0]),
        pltpu.make_async_copy(dy_ref, db.at[pl.ds(OWN, ROWS)], loc_sem.at[1]),
        pltpu.make_async_copy(wu_ref.at[0], wu.at[:, pl.ds(0, hid_n)], loc_sem.at[2]),
        pltpu.make_async_copy(wd_ref.at[0], wd.at[:, pl.ds(0, hid_n)], loc_sem.at[3]),
    ]
    for copy in own:
        copy.start()
    names = lax.broadcasted_iota(jnp.int32, (EXP, ROWS), 0)
    dense = jnp.zeros((EXP, ROWS), F32)
    for k in range(ids_ref.shape[0]):
        dense = dense + jnp.where(ids_ref[k : k + 1, :] == names, gates_ref[k : k + 1, :].astype(F32), 0.0)
    gt[NZ - 2] = dense.astype(BF16)
    pl.semaphore_wait(barrier, len(partners))

    def remote(src, dst, ssem, rsem, device):
        return pltpu.make_async_remote_copy(
            src_ref=src, dst_ref=dst, send_sem=ssem, recv_sem=rsem,
            device_id=device, device_id_type=MESH,
        )

    bufs = (xb, db)
    last_way = (0, 1, 0)

    def block(arr, k):
        if arr == 2:
            return gt.at[k]
        return bufs[arr].at[pl.ds(k * ROWS, ROWS)]

    def slot(s, r):
        return NZ - 1 if s == 4 else 2 * (s - 1) + r

    sent = []

    def send_block(arr, r, s, src):
        copy = remote(src, block(arr, slot(s, r)), ag_send.at[arr, r, s - 1], ag_recv.at[arr, r, s], zdev[r])
        copy.start()
        sent.append(copy)

    def arrive(arr, s):
        for r in range(2):
            if s == 4 and last_way[arr] != r:
                continue
            here = block(arr, slot(s, r))
            remote(here, here, ag_send.at[arr, r, 0], ag_recv.at[arr, r, s], zdev[r]).wait_recv()
            if s < 3 or (s == 3 and last_way[arr] == r):
                send_block(arr, r, s + 1, here)

    for arr, src in ((0, x_ref), (1, dy_ref), (2, gt.at[NZ - 2])):
        for r in range(2):
            send_block(arr, r, 1, src)
    part = width // 2
    weight_first, weight_core, weight_relay = [], [], []
    for h in range(2):
        for m, (src, buf, far) in enumerate(((wu_ref, wu, y_pair), (wd_ref, wd, y_other))):
            rows = pl.ds(h * part, part)
            lanes = [pl.ds(j * hid_n, hid_n) for j in range(4)]
            weight_first.append(remote(
                src.at[0, rows], buf.at[rows, lanes[1]], w_send.at[m, h, 0], w_recv.at[m, h, 0], far))
            weight_core.append(remote(
                src.at[0, rows], buf.at[rows, lanes[2]], w_send.at[m, h, 1], w_recv.at[m, h, 1], cdev))
            weight_relay.append(remote(
                buf.at[rows, lanes[1]], buf.at[rows, lanes[3]], w_send.at[m, h, 2], w_recv.at[m, h, 2], cdev))
    for copy in weight_first + weight_core:
        copy.start()

    lane = lax.broadcasted_iota(jnp.int32, (1, LANES), 1)
    lane32 = lax.broadcasted_iota(jnp.int32, (1, EXP), 1)
    chunk = 32
    slots = [((yl if j % 2 == 0 else 1 - yl) * NZ + z) * 2 + (core if j < 2 else 1 - core) for j in range(4)]

    def compute(k, blocks):
        base, size = k * ROWS, blocks * ROWS
        rows = pl.ds(base, size)
        for b in range(blocks):
            gs[pl.ds(b * ROWS, ROWS), :] = gt[k + b].astype(F32).T

        def hidden_part(n, carry):
            at = pl.ds(pl.multiple_of(n * 512, 512), 512)
            pre_s[:size, at] = jnp.dot(xb[rows, :], wu[:, at], preferred_element_type=F32)
            bh_s[:size, at] = jnp.dot(db[rows, :], wd[:, at], preferred_element_type=F32)
            return carry

        lax.fori_loop(0, 4 * hid_n // 512, hidden_part, 0)

        def piece(q, carry):
            at = pl.multiple_of(q * chunk, chunk)
            sub = pl.ds(at, chunk)
            big = pl.ds(pl.multiple_of(base + at, chunk), chunk)
            out = jnp.zeros((chunk, LANES), F32)
            for j in range(4):
                lanes = pl.ds(j * hid_n, hid_n)
                g = jnp.sum(jnp.where(lane32 == slots[j], gs[sub, :], 0.0), axis=1, keepdims=True)
                pre, bh = pre_s[sub, lanes], bh_s[sub, lanes]
                sig = 0.5 * jnp.tanh(0.5 * pre) + 0.5
                hidden = (pre * sig).astype(BF16).astype(F32)
                gate = jnp.sum(bh * hidden, axis=1, keepdims=True)
                slope = sig * (1.0 + pre * (1.0 - sig))
                gp[sub, lanes] = (g * bh * slope).astype(BF16)
                gh[big, lanes] = (g * hidden).astype(BF16)
                out = jnp.where(lane == slots[j], gate, out)
            gq[sub, :] = out
            return carry

        lax.fori_loop(0, size // chunk, piece, 0)
        for b in range(blocks):
            pg[k + b] = gq[pl.ds(b * ROWS, ROWS), :].T[:EXP, :].astype(BF16)

        def columns(t, carry):
            at = pl.ds(pl.multiple_of(t * 512, 512), 512)
            pb[rows, at] = lax.dot_general(
                gp[:size, :], wu[at, :], (((1,), (1,)), ((), ())), preferred_element_type=F32).astype(BF16)
            return carry

        lax.fori_loop(0, width // 512, columns, 0)

    def core_copy(q, part):
        src, dst = ((s1.at[q], r1.at[q]), (s2.at[:, q], r2.at[:, q]))[part]
        return remote(src, dst, c_send.at[q, part], c_recv.at[q, part], cdev)

    deep = NZ * ROWS // 2

    def down_tile(phase):
        def body(q, carry):
            d = jnp.where(q == 0, 2, jnp.where(q == 3, 0, jnp.where(q == 2, 3, 1)))
            at = pl.ds(pl.multiple_of(lax.rem(x + d, NX) * tile, tile), tile)
            for k in range(deep // ROWS):
                dyt[:, pl.ds(k * ROWS, ROWS)] = db[pl.ds(phase * deep + k * ROWS, ROWS), at].T
            rows = pl.ds(phase * deep, deep)
            for by_x, by_y, start in ((s1, s2, 2 * hid_n), (a1, a2, 0)):
                term = jnp.dot(dyt[...], gh[rows, pl.ds(start, 2 * hid_n)], preferred_element_type=F32)
                for jj in range(2):
                    for row in range(NYH):
                        top = row * ROWS
                        upper = term[top : top + MID, jj * hid_n : (jj + 1) * hid_n]
                        lower = term[top + MID : top + ROWS, jj * hid_n : (jj + 1) * hid_n]
                        k = lax.rem(2 * row + (yl if jj == 0 else 1 - yl) + NY - yy, NY)
                        if phase:
                            upper = upper + by_x[q, jj, row].astype(F32)
                            lower = lower + by_y[k, q].astype(F32)
                        by_x[q, jj, row] = upper.astype(BF16)
                        by_y[k, q] = lower.astype(BF16)
            if phase:
                for half in range(2):
                    core_copy(q, half).start()
            return carry
        return body

    cols = (pl.ds(0, HALF), pl.ds(HALF, width - HALF))
    back = (zdev[1], zdev[0])

    def rs_copy(r, t, h):
        k = slot(4 - t, r)
        if h == 2:
            src, dst = pg.at[k], rg.at[r, t]
        else:
            src, dst = pb.at[pl.ds(k * ROWS, ROWS), cols[h]], rb.at[r, t, :, cols[h]]
        return remote(src, dst, rs_send.at[r, t, h], rs_recv.at[r, t, h], back[r])

    def rs_add(r, t, h):
        rs_copy(r, t - 1, h).wait_recv()
        k = slot(4 - t, r)
        if h == 2:
            pg[k] = (pg[k].astype(F32) + rg[r, t - 1].astype(F32)).astype(BF16)
        else:
            row = pl.ds(k * ROWS, ROWS)
            pb[row, cols[h]] = (
                pb[row, cols[h]].astype(F32) + rb[r, t - 1, :, cols[h]].astype(F32)).astype(BF16)
        rs_copy(r, t, h).start()

    def rs_free(t):
        for r in range(2):
            rs_add(r, t, 1 - r)

    def rs_tied(t):
        for r in range(2):
            rs_add(r, t, r)
        for r in range(2):
            if t > 1 or r == 0:
                rs_add(r, t, 2)

    for arr in (0, 1, 2):
        arrive(arr, 1)
    for first, relay in zip(weight_first, weight_relay):
        first.wait_recv()
        relay.start()
    for copy in own:
        copy.wait()
    for copy in weight_core + weight_relay:
        copy.wait_recv()
    compute(NZ - 2, 1)
    arrive(0, 2)
    compute(0, 2)
    arrive(1, 2)
    arrive(2, 2)
    compute(2, 2)
    arrive(0, 3)
    lax.fori_loop(0, NX, down_tile(0), 0)
    arrive(1, 3)
    arrive(2, 3)
    compute(4, 2)
    for r in range(2):
        rs_copy(r, 1, 1 - r).start()
    rs_copy(1, 1, 2).start()
    for arr in (0, 1, 2):
        arrive(arr, 4)
    compute(NZ - 1, 1)
    for r in range(2):
        rs_copy(r, 0, r).start()
    rs_copy(0, 0, 2).start()
    lax.fori_loop(0, 2, down_tile(1), 0)
    rs_free(2)
    lax.fori_loop(2, NX, down_tile(1), 0)

    def add_into(dst, *others):
        total = dst[...].astype(F32)
        for other in others:
            total = total + other[...].astype(F32)
        dst[...] = total.astype(BF16)

    class Ring:
        def __init__(self, n, piece, recv, sems, devices):
            self.n, self.piece, self.recv, self.sems, self.devices = n, piece, recv, sems, devices
            self.started = []

        def copy(self, r, t, h):
            m = self.n // 2 - t
            return remote(
                self.piece(m if r == 0 else self.n - m, h), self.recv.at[r, t, h],
                self.sems.at[0, r, t, h], self.sems.at[1, r, t, h], self.devices[r])

        def send(self, r, t, h):
            self.copy(r, t, h).start()
            self.started.append((r, t, h))

        def begin(self):
            for r in range(2):
                self.send(r, 0, r)

        def forward(self, t, free):
            for r in range(2):
                h = 1 - r if free else r
                if t > 1 or not free:
                    m = self.n // 2 - t
                    self.copy(r, t - 1, h).wait_recv()
                    add_into(self.piece(m if r == 0 else self.n - m, h), self.recv.at[r, t - 1, h])
                self.send(r, t, h)

        def finish(self):
            t = self.n // 2 - 1
            for free in (1, 0):
                for r in range(2):
                    self.copy(r, t, 1 - r if free else r).wait_recv()
            for h in range(2):
                add_into(self.piece(0, h), self.recv.at[0, t, h], self.recv.at[1, t, h])

        def drain(self):
            for r, t, h in self.started:
                self.copy(r, t, h).wait_send()

    place = {2: 0, 1: 1, NX - 1: 2, 0: 3}
    sub = MID // 2

    def y_row(k):
        return lax.rem(yy + k, NY) // 2

    ring_x1 = Ring(NX, lambda k, h: a1.at[place[k], h], rx1, x_sems, xdev)
    ring_y1 = Ring(NY, lambda k, h: a1.at[3, k % 2, y_row(k), pl.ds(h * sub, sub)], ry1, y1_sems, ydev)
    ring_y2 = Ring(NY, lambda k, h: a2.at[k, pl.ds(2 * h, 2)], ry2, y2_sems, ydev)
    ring_x2 = Ring(NX, lambda k, h: a2.at[0, place[k], pl.ds(h * sub, sub)], rx2, x2_sems, xdev)

    for q in range(3):
        core_copy(q, 0).wait_recv()
        for jj in range(2):
            add_into(a1.at[q, jj], r1.at[q, jj])
        if q == 0:
            ring_x1.begin()
    ring_x1.forward(1, True)
    for q in range(NX):
        core_copy(q, 1).wait_recv()
    for k in (NY // 2, 3, 5):
        add_into(a2.at[k], r2.at[k])
        if k == NY // 2:
            ring_y2.begin()
    ring_y2.forward(1, True)
    rs_tied(1)
    for k in (2, 6, 1, 7, 0):
        add_into(a2.at[k], r2.at[k])
    core_copy(3, 0).wait_recv()
    for jj in range(2):
        add_into(a1.at[3, jj], r1.at[3, jj])
    ring_y2.forward(1, False)
    ring_x1.forward(1, False)
    ring_y2.forward(2, True)
    rs_free(3)
    ring_y2.forward(2, False)
    ring_y2.forward(3, True)
    rs_tied(2)
    ring_x1.finish()
    ring_y1.begin()
    ring_y1.forward(1, True)
    ring_y2.forward(3, False)
    ring_y1.forward(2, True)
    ring_y1.forward(1, False)
    ring_y2.finish()
    ring_x2.begin()
    ring_x2.forward(1, True)
    ring_y1.forward(3, True)
    ring_y1.forward(2, False)
    ring_x2.forward(1, False)
    rs_tied(3)
    ring_y1.forward(3, False)
    ring_x2.finish()
    dg_ref[MID:, :] = a2[0, 3].astype(F32)
    ring_y1.finish()
    dg_ref[:MID, :] = a1[3, 0, yh].astype(F32)

    mine = pl.ds(OWN, ROWS)
    for h in (1, 0):
        for r in range(2):
            rs_copy(r, 3, r ^ h).wait_recv()
    for h in range(2):
        tok_ref[:, cols[h]] = (
            pb[mine, cols[h]].astype(F32) + rb[0, 3, :, cols[h]].astype(F32) + rb[1, 3, :, cols[h]].astype(F32)
        ).astype(BF16)
    for r in range(2):
        rs_copy(r, 3, 2).wait_recv()
    gates = pg[NZ - 2].astype(F32) + rg[0, 3].astype(F32) + rg[1, 3].astype(F32)
    for k in range(ids_ref.shape[0]):
        picked = jnp.where(ids_ref[k : k + 1, :] == names, gates, 0.0)
        gg_ref[k : k + 1, :] = jnp.sum(picked, axis=0, keepdims=True)

    for copy in sent + weight_first + weight_core + weight_relay:
        copy.wait_send()
    for r in range(2):
        for t in range(4):
            for h in range(3):
                if t == 0 and h != (r if h < 2 else 2 + r):
                    continue
                rs_copy(r, t, h).wait_send()
    for q in range(NX):
        for half in range(2):
            core_copy(q, half).wait_send()
    for ring in (ring_x1, ring_y1, ring_y2, ring_x2):
        ring.drain()


def finish(tok_ref, gates_ref, down_ref, tok_out, gates_out, down_out):
    tok_out[...] = tok_ref[...]
    gates_out[...] = gates_ref[...].astype(BF16)
    down_out[...] = down_ref[...]


def shards(tokens, cotangent, expert_ids, gate_weights, w_up, w_down):
    rows, width = tokens.shape
    hid_n = w_up.shape[2]
    tile = width // NX
    dma, vmem = pltpu.SemaphoreType.DMA, pltpu.VMEM
    hbm = pl.BlockSpec(memory_space=pl.ANY)
    local = pl.BlockSpec(memory_space=pltpu.VMEM)
    token_grad, gates, down = pl.pallas_call(
        kernel,
        out_shape=(
            jax.ShapeDtypeStruct((rows, width), BF16),
            jax.ShapeDtypeStruct((expert_ids.shape[1], rows), F32),
            jax.ShapeDtypeStruct((width // (NX * NYH), hid_n), F32),
        ),
        in_specs=[hbm] * 4 + [local] * 2,
        out_specs=[local] * 3,
        scratch_shapes=[
            vmem((NZ * rows, width), BF16),
            vmem((NZ * rows, width), BF16),
            vmem((NZ, EXP, rows), BF16),
            vmem((width, 4 * hid_n), BF16),
            vmem((width, 4 * hid_n), BF16),
            vmem((NZ * rows, 4 * hid_n), BF16),
            vmem((2 * rows, 4 * hid_n), BF16),
            vmem((2 * rows, 4 * hid_n), F32),
            vmem((2 * rows, 4 * hid_n), F32),
            vmem((2 * rows, EXP), F32),
            vmem((2 * rows, LANES), F32),
            vmem((NZ * rows, width), BF16),
            vmem((NZ, EXP, rows), BF16),
            vmem((2, 4, rows, width), BF16),
            vmem((2, 4, EXP, rows), BF16),
            vmem((tile, NZ * rows // 2), BF16),
            vmem((NX, 2, NYH, MID, hid_n), BF16),
            vmem((NY, NX, MID, hid_n), BF16),
            vmem((NX, 2, NYH, MID, hid_n), BF16),
            vmem((NY, NX, MID, hid_n), BF16),
            vmem((NX, 2, NYH, MID, hid_n), BF16),
            vmem((NY, NX, MID, hid_n), BF16),
            vmem((2, 2, 2, NYH, MID, hid_n), BF16),
            vmem((2, 4, 2, MID // 2, hid_n), BF16),
            vmem((2, 4, 2, 2, MID, hid_n), BF16),
            vmem((2, 2, 2, MID // 2, hid_n), BF16),
            dma((4,)),
            dma((3, 2, 4)),
            dma((3, 2, 5)),
            dma((2, 2, 3)),
            dma((2, 2, 3)),
            dma((2, 4, 3)),
            dma((2, 4, 3)),
            dma((NX, 2)),
            dma((NX, 2)),
            dma((2, 2, 2, 2)),
            dma((2, 2, 4, 2)),
            dma((2, 2, 4, 2)),
            dma((2, 2, 2, 2)),
        ],
        compiler_params=pltpu.CompilerParams(
            collective_id=0, has_side_effects=True, vmem_limit_bytes=66_000_000
        ),
        name="expert_backward",
    )(tokens, cotangent, w_up, w_down, expert_ids.T, gate_weights.T)
    token_grad, gates, down = pl.pallas_call(
        finish,
        out_shape=(
            jax.ShapeDtypeStruct(token_grad.shape, BF16),
            jax.ShapeDtypeStruct(gates.shape, BF16),
            jax.ShapeDtypeStruct(down.shape, F32),
        ),
        in_specs=[local] * 3,
        out_specs=[local] * 3,
        name="finish",
    )(token_grad, gates, down)
    return token_grad, gates.T, down[None]


def solution(mesh):
    return jax.shard_map(
        shards,
        mesh=mesh,
        in_specs=(
            P(("dp", "ep"), None),
            P(("dp", "ep"), None),
            P(("dp", "ep"), None),
            P(("dp", "ep"), None),
            P("ep", None, None),
            P("ep", None, None),
        ),
        out_specs=(P(("dp", "ep"), None), P(("dp", "ep"), None), P("ep", "dp", None)),
        check_vma=False,
    )
```

```python
import jax
import jax.numpy as jnp
from jax import lax
from jax.experimental import pallas as pl
from jax.experimental.pallas import tpu as pltpu
from jax.sharding import PartitionSpec as P

MESH = pl.DeviceIdType.MESH
BF16, F32 = jnp.bfloat16, jnp.float32
NX, NYH, NZ = 4, 4, 8
NY = 2 * NYH
ROWS = 128
LANES = 128
QUART = 512
EXP = 32
MID = 64


def kernel(
    x_ref, dy_ref, wu_ref, wd_ref, ids_ref, gates_ref, tok_ref, gg_ref, dg_ref,
    xb, db, gt, wu, wd, gh, gp, pre_s, bh_s, gs, gq, pb, pg, rb, rg, dyt, a1, a2, s1, s2, r1, r2, rx1, ry1, ry2, rx2,
    loc_sem, ag_send, ag_recv, w_send, w_recv, rs_send, rs_recv, c_send, c_recv, x_sems, y1_sems, y2_sems, x2_sems,
):
    width = dy_ref.shape[1]
    hid_n = wu_ref.shape[2]
    tile = width // NX
    dp, ep = lax.axis_index("dp"), lax.axis_index("ep")
    core = lax.rem(ep, 2)
    z = lax.rem(ep // 2, NZ)
    yl = ep // (2 * NZ)
    x, yh = dp // NYH, lax.rem(dp, NYH)
    yy = 2 * yh + yl

    def dev(x_, y_, z_, c_):
        return (x_ * NYH + y_ // 2, (lax.rem(y_, 2) * NZ + z_) * 2 + c_)

    zdev = [dev(x, yy, lax.rem(z + 1, NZ), core), dev(x, yy, lax.rem(z + NZ - 1, NZ), core)]
    cdev = dev(x, yy, z, 1 - core)
    ydev = [dev(x, lax.rem(yy + 1, NY), z, core), dev(x, lax.rem(yy + NY - 1, NY), z, core)]
    y_pair = dev(x, lax.rem(yy + NY + 1 - 2 * yl, NY), z, core)
    y_other = dev(x, lax.rem(yy + NY + 2 * yl - 1, NY), z, core)
    xdev = [dev(lax.rem(x + 1, NX), yy, z, core), dev(lax.rem(x + NX - 1, NX), yy, z, core)]

    barrier = pltpu.get_barrier_semaphore()
    partners = zdev + [cdev] + ydev + xdev
    for device in partners:
        pl.semaphore_signal(barrier, inc=1, device_id=device, device_id_type=MESH)

    OWN, FAR = (NZ - 2) * ROWS, (NZ - 1) * ROWS
    own = [
        pltpu.make_async_copy(x_ref, xb.at[pl.ds(OWN, ROWS)], loc_sem.at[0]),
        pltpu.make_async_copy(dy_ref, db.at[pl.ds(OWN, ROWS)], loc_sem.at[1]),
        pltpu.make_async_copy(wu_ref.at[0], wu.at[:, pl.ds(0, hid_n)], loc_sem.at[2]),
        pltpu.make_async_copy(wd_ref.at[0], wd.at[:, pl.ds(0, hid_n)], loc_sem.at[3]),
    ]
    for copy in own:
        copy.start()
    names = lax.broadcasted_iota(jnp.int32, (EXP, ROWS), 0)
    dense = jnp.zeros((EXP, ROWS), F32)
    for k in range(ids_ref.shape[0]):
        dense = dense + jnp.where(ids_ref[k : k + 1, :] == names, gates_ref[k : k + 1, :].astype(F32), 0.0)
    gt[NZ - 2] = dense.astype(BF16)
    pl.semaphore_wait(barrier, len(partners))

    def remote(src, dst, ssem, rsem, device):
        return pltpu.make_async_remote_copy(
            src_ref=src, dst_ref=dst, send_sem=ssem, recv_sem=rsem,
            device_id=device, device_id_type=MESH,
        )

    bufs = (xb, db)
    last_way = (0, 1, 0)

    def block(arr, k):
        if arr == 2:
            return gt.at[k]
        return bufs[arr].at[pl.ds(k * ROWS, ROWS)]

    def slot(s, r):
        return NZ - 1 if s == 4 else 2 * (s - 1) + r

    sent = []

    def send_block(arr, r, s, src):
        copy = remote(src, block(arr, slot(s, r)), ag_send.at[arr, r, s - 1], ag_recv.at[arr, r, s], zdev[r])
        copy.start()
        sent.append(copy)

    def arrive(arr, s):
        for r in range(2):
            if s == 4 and last_way[arr] != r:
                continue
            here = block(arr, slot(s, r))
            remote(here, here, ag_send.at[arr, r, 0], ag_recv.at[arr, r, s], zdev[r]).wait_recv()
            if s < 3 or (s == 3 and last_way[arr] == r):
                send_block(arr, r, s + 1, here)

    for arr, src in ((0, x_ref), (1, dy_ref), (2, gt.at[NZ - 2])):
        for r in range(2):
            send_block(arr, r, 1, src)
    part = width // 2
    weight_first, weight_core, weight_relay = [], [], []
    for h in range(2):
        for m, (src, buf, far) in enumerate(((wu_ref, wu, y_pair), (wd_ref, wd, y_other))):
            rows = pl.ds(h * part, part)
            lanes = [pl.ds(j * hid_n, hid_n) for j in range(4)]
            weight_first.append(remote(
                src.at[0, rows], buf.at[rows, lanes[1]], w_send.at[m, h, 0], w_recv.at[m, h, 0], far))
            weight_core.append(remote(
                src.at[0, rows], buf.at[rows, lanes[2]], w_send.at[m, h, 1], w_recv.at[m, h, 1], cdev))
            weight_relay.append(remote(
                buf.at[rows, lanes[1]], buf.at[rows, lanes[3]], w_send.at[m, h, 2], w_recv.at[m, h, 2], cdev))
    for copy in weight_first + weight_core:
        copy.start()

    lane = lax.broadcasted_iota(jnp.int32, (1, LANES), 1)
    lane32 = lax.broadcasted_iota(jnp.int32, (1, EXP), 1)
    chunk = 32
    slots = [((yl if j % 2 == 0 else 1 - yl) * NZ + z) * 2 + (core if j < 2 else 1 - core) for j in range(4)]

    def compute(k, blocks):
        base, size = k * ROWS, blocks * ROWS
        rows = pl.ds(base, size)
        for b in range(blocks):
            gs[pl.ds(b * ROWS, ROWS), :] = gt[k + b].astype(F32).T

        def hidden_part(n, carry):
            at = pl.ds(pl.multiple_of(n * 512, 512), 512)
            pre_s[:size, at] = jnp.dot(xb[rows, :], wu[:, at], preferred_element_type=F32)
            bh_s[:size, at] = jnp.dot(db[rows, :], wd[:, at], preferred_element_type=F32)
            return carry

        lax.fori_loop(0, 4 * hid_n // 512, hidden_part, 0)

        def piece(q, carry):
            at = pl.multiple_of(q * chunk, chunk)
            sub = pl.ds(at, chunk)
            big = pl.ds(pl.multiple_of(base + at, chunk), chunk)
            out = jnp.zeros((chunk, LANES), F32)
            for j in range(4):
                lanes = pl.ds(j * hid_n, hid_n)
                g = jnp.sum(jnp.where(lane32 == slots[j], gs[sub, :], 0.0), axis=1, keepdims=True)
                pre, bh = pre_s[sub, lanes], bh_s[sub, lanes]
                sig = 0.5 * jnp.tanh(0.5 * pre) + 0.5
                hidden = (pre * sig).astype(BF16).astype(F32)
                gate = jnp.sum(bh * hidden, axis=1, keepdims=True)
                slope = sig * (1.0 + pre * (1.0 - sig))
                gp[sub, lanes] = (g * bh * slope).astype(BF16)
                gh[big, lanes] = (g * hidden).astype(BF16)
                out = jnp.where(lane == slots[j], gate, out)
            gq[sub, :] = out
            return carry

        lax.fori_loop(0, size // chunk, piece, 0)
        for b in range(blocks):
            pg[k + b] = gq[pl.ds(b * ROWS, ROWS), :].T[:EXP, :].astype(BF16)

        def columns(t, carry):
            at = pl.ds(pl.multiple_of(t * 512, 512), 512)
            pb[rows, at] = lax.dot_general(
                gp[:size, :], wu[at, :], (((1,), (1,)), ((), ())), preferred_element_type=F32).astype(BF16)
            return carry

        lax.fori_loop(0, width // 512, columns, 0)

    def core_copy(q, part):
        src, dst = ((s1.at[q], r1.at[q]), (s2.at[:, q], r2.at[:, q]))[part]
        return remote(src, dst, c_send.at[q, part], c_recv.at[q, part], cdev)

    deep = NZ * ROWS // 2

    def down_tile(phase):
        def body(q, carry):
            d = jnp.where(q == 0, 2, jnp.where(q == 3, 0, jnp.where(q == 2, 3, 1)))
            at = pl.ds(pl.multiple_of(lax.rem(x + d, NX) * tile, tile), tile)
            for k in range(deep // ROWS):
                dyt[:, pl.ds(k * ROWS, ROWS)] = db[pl.ds(phase * deep + k * ROWS, ROWS), at].T
            rows = pl.ds(phase * deep, deep)
            for by_x, by_y, start in ((s1, s2, 2 * hid_n), (a1, a2, 0)):
                term = jnp.dot(dyt[...], gh[rows, pl.ds(start, 2 * hid_n)], preferred_element_type=F32)
                for jj in range(2):
                    for row in range(NYH):
                        top = row * ROWS
                        upper = term[top : top + MID, jj * hid_n : (jj + 1) * hid_n]
                        lower = term[top + MID : top + ROWS, jj * hid_n : (jj + 1) * hid_n]
                        k = lax.rem(2 * row + (yl if jj == 0 else 1 - yl) + NY - yy, NY)
                        if phase:
                            upper = upper + by_x[q, jj, row].astype(F32)
                            lower = lower + by_y[k, q].astype(F32)
                        by_x[q, jj, row] = upper.astype(BF16)
                        by_y[k, q] = lower.astype(BF16)
            if phase:
                for half in range(2):
                    core_copy(q, half).start()
            return carry
        return body

    cols = [pl.ds(c * QUART, QUART) for c in range(4)]
    GATES = 4
    back = (zdev[1], zdev[0])

    def rs_copy(r, t, h):
        k = slot(4 - t, r)
        if h == GATES:
            src, dst = pg.at[k], rg.at[r, t]
        else:
            src, dst = pb.at[pl.ds(k * ROWS, ROWS), cols[h]], rb.at[r, t, :, cols[h]]
        return remote(src, dst, rs_send.at[r, t, h], rs_recv.at[r, t, h], back[r])

    def rs_add(r, t, h):
        rs_copy(r, t - 1, h).wait_recv()
        k = slot(4 - t, r)
        if h == GATES:
            pg[k] = (pg[k].astype(F32) + rg[r, t - 1].astype(F32)).astype(BF16)
        else:
            row = pl.ds(k * ROWS, ROWS)
            pb[row, cols[h]] = (
                pb[row, cols[h]].astype(F32) + rb[r, t - 1, :, cols[h]].astype(F32)).astype(BF16)
        rs_copy(r, t, h).start()

    def rs_free(t):
        for c in range(2):
            for r in range(2):
                rs_add(r, t, 2 * (1 - r) + c)

    def rs_tied(t, parts=(0, 1)):
        for c in parts:
            for r in range(2):
                rs_add(r, t, 2 * r + c)
        if 1 in parts:
            for r in range(2):
                if t > 1 or r == 0:
                    rs_add(r, t, GATES)

    for arr in (0, 1, 2):
        arrive(arr, 1)
    for first, relay in zip(weight_first, weight_relay):
        first.wait_recv()
        relay.start()
    for copy in own:
        copy.wait()
    for copy in weight_core + weight_relay:
        copy.wait_recv()
    compute(NZ - 2, 1)
    arrive(0, 2)
    compute(0, 2)
    arrive(1, 2)
    arrive(2, 2)
    compute(2, 2)
    arrive(0, 3)
    lax.fori_loop(0, NX, down_tile(0), 0)
    arrive(1, 3)
    arrive(2, 3)
    compute(4, 2)
    for c in range(2):
        for r in range(2):
            rs_copy(r, 1, 2 * (1 - r) + c).start()
    rs_copy(1, 1, GATES).start()
    for arr in (0, 1, 2):
        arrive(arr, 4)
    compute(NZ - 1, 1)
    for c in range(2):
        for r in range(2):
            rs_copy(r, 0, 2 * r + c).start()
    rs_copy(0, 0, GATES).start()
    lax.fori_loop(0, 2, down_tile(1), 0)
    rs_free(2)
    lax.fori_loop(2, NX, down_tile(1), 0)

    def add_into(dst, *others):
        total = dst[...].astype(F32)
        for other in others:
            total = total + other[...].astype(F32)
        dst[...] = total.astype(BF16)

    class Ring:
        def __init__(self, n, piece, recv, sems, devices):
            self.n, self.piece, self.recv, self.sems, self.devices = n, piece, recv, sems, devices
            self.started = []

        def copy(self, r, t, h):
            m = self.n // 2 - t
            return remote(
                self.piece(m if r == 0 else self.n - m, h), self.recv.at[r, t, h],
                self.sems.at[0, r, t, h], self.sems.at[1, r, t, h], self.devices[r])

        def send(self, r, t, h):
            self.copy(r, t, h).start()
            self.started.append((r, t, h))

        def begin(self):
            for r in range(2):
                self.send(r, 0, r)

        def forward(self, t, free):
            for r in range(2):
                h = 1 - r if free else r
                if t > 1 or not free:
                    m = self.n // 2 - t
                    self.copy(r, t - 1, h).wait_recv()
                    add_into(self.piece(m if r == 0 else self.n - m, h), self.recv.at[r, t - 1, h])
                self.send(r, t, h)

        def finish(self):
            t = self.n // 2 - 1
            for free in (1, 0):
                for r in range(2):
                    self.copy(r, t, 1 - r if free else r).wait_recv()
            for h in range(2):
                add_into(self.piece(0, h), self.recv.at[0, t, h], self.recv.at[1, t, h])

        def drain(self):
            for r, t, h in self.started:
                self.copy(r, t, h).wait_send()

    place = {2: 0, 1: 1, NX - 1: 2, 0: 3}
    sub = MID // 2

    def y_row(k):
        return lax.rem(yy + k, NY) // 2

    ring_x1 = Ring(NX, lambda k, h: a1.at[place[k], h], rx1, x_sems, xdev)
    ring_y1 = Ring(NY, lambda k, h: a1.at[3, k % 2, y_row(k), pl.ds(h * sub, sub)], ry1, y1_sems, ydev)
    ring_y2 = Ring(NY, lambda k, h: a2.at[k, pl.ds(2 * h, 2)], ry2, y2_sems, ydev)
    ring_x2 = Ring(NX, lambda k, h: a2.at[0, place[k], pl.ds(h * sub, sub)], rx2, x2_sems, xdev)

    for q in range(3):
        core_copy(q, 0).wait_recv()
        for jj in range(2):
            add_into(a1.at[q, jj], r1.at[q, jj])
        if q == 0:
            ring_x1.begin()
    ring_x1.forward(1, True)
    for q in range(NX):
        core_copy(q, 1).wait_recv()
    for k in (NY // 2, 3, 5):
        add_into(a2.at[k], r2.at[k])
        if k == NY // 2:
            ring_y2.begin()
    ring_y2.forward(1, True)
    rs_tied(1)
    for k in (2, 6, 1, 7, 0):
        add_into(a2.at[k], r2.at[k])
    core_copy(3, 0).wait_recv()
    for jj in range(2):
        add_into(a1.at[3, jj], r1.at[3, jj])
    ring_y2.forward(1, False)
    ring_x1.forward(1, False)
    ring_y2.forward(2, True)
    rs_free(3)
    ring_y2.forward(2, False)
    ring_y2.forward(3, True)
    rs_tied(2)
    ring_x1.finish()
    ring_y1.begin()
    ring_y1.forward(1, True)
    ring_y2.forward(3, False)
    ring_y1.forward(2, True)
    ring_y1.forward(1, False)
    rs_tied(3, (0,))
    ring_y2.finish()
    ring_x2.begin()
    ring_x2.forward(1, True)
    ring_y1.forward(3, True)
    ring_y1.forward(2, False)
    rs_tied(3, (1,))
    ring_x2.forward(1, False)
    ring_y1.forward(3, False)
    ring_x2.finish()
    dg_ref[MID:, :] = a2[0, 3].astype(F32)
    ring_y1.finish()
    dg_ref[:MID, :] = a1[3, 0, yh].astype(F32)

    mine = pl.ds(OWN, ROWS)
    for h in (0, 2, 1, 3):
        for r in range(2):
            rs_copy(r, 3, h).wait_recv()
        tok_ref[:, cols[h]] = (
            pb[mine, cols[h]].astype(F32) + rb[0, 3, :, cols[h]].astype(F32) + rb[1, 3, :, cols[h]].astype(F32)
        ).astype(BF16)
    for r in range(2):
        rs_copy(r, 3, GATES).wait_recv()
    gates = pg[NZ - 2].astype(F32) + rg[0, 3].astype(F32) + rg[1, 3].astype(F32)
    for k in range(ids_ref.shape[0]):
        picked = jnp.where(ids_ref[k : k + 1, :] == names, gates, 0.0)
        gg_ref[k : k + 1, :] = jnp.sum(picked, axis=0, keepdims=True)

    for copy in sent + weight_first + weight_core + weight_relay:
        copy.wait_send()
    for r in range(2):
        for t in range(4):
            for h in range(5):
                if t == 0 and h not in ((0, 1, GATES) if r == 0 else (2, 3)):
                    continue
                rs_copy(r, t, h).wait_send()
    for q in range(NX):
        for half in range(2):
            core_copy(q, half).wait_send()
    for ring in (ring_x1, ring_y1, ring_y2, ring_x2):
        ring.drain()


def finish(tok_ref, gates_ref, down_ref, tok_out, gates_out, down_out):
    tok_out[...] = tok_ref[...]
    gates_out[...] = gates_ref[...].astype(BF16)
    down_out[...] = down_ref[...]


def shards(tokens, cotangent, expert_ids, gate_weights, w_up, w_down):
    rows, width = tokens.shape
    hid_n = w_up.shape[2]
    tile = width // NX
    dma, vmem = pltpu.SemaphoreType.DMA, pltpu.VMEM
    hbm = pl.BlockSpec(memory_space=pl.ANY)
    local = pl.BlockSpec(memory_space=pltpu.VMEM)
    token_grad, gates, down = pl.pallas_call(
        kernel,
        out_shape=(
            jax.ShapeDtypeStruct((rows, width), BF16),
            jax.ShapeDtypeStruct((expert_ids.shape[1], rows), F32),
            jax.ShapeDtypeStruct((width // (NX * NYH), hid_n), F32),
        ),
        in_specs=[hbm] * 4 + [local] * 2,
        out_specs=[local] * 3,
        scratch_shapes=[
            vmem((NZ * rows, width), BF16),
            vmem((NZ * rows, width), BF16),
            vmem((NZ, EXP, rows), BF16),
            vmem((width, 4 * hid_n), BF16),
            vmem((width, 4 * hid_n), BF16),
            vmem((NZ * rows, 4 * hid_n), BF16),
            vmem((2 * rows, 4 * hid_n), BF16),
            vmem((2 * rows, 4 * hid_n), F32),
            vmem((2 * rows, 4 * hid_n), F32),
            vmem((2 * rows, EXP), F32),
            vmem((2 * rows, LANES), F32),
            vmem((NZ * rows, width), BF16),
            vmem((NZ, EXP, rows), BF16),
            vmem((2, 4, rows, width), BF16),
            vmem((2, 4, EXP, rows), BF16),
            vmem((tile, NZ * rows // 2), BF16),
            vmem((NX, 2, NYH, MID, hid_n), BF16),
            vmem((NY, NX, MID, hid_n), BF16),
            vmem((NX, 2, NYH, MID, hid_n), BF16),
            vmem((NY, NX, MID, hid_n), BF16),
            vmem((NX, 2, NYH, MID, hid_n), BF16),
            vmem((NY, NX, MID, hid_n), BF16),
            vmem((2, 2, 2, NYH, MID, hid_n), BF16),
            vmem((2, 4, 2, MID // 2, hid_n), BF16),
            vmem((2, 4, 2, 2, MID, hid_n), BF16),
            vmem((2, 2, 2, MID // 2, hid_n), BF16),
            dma((4,)),
            dma((3, 2, 4)),
            dma((3, 2, 5)),
            dma((2, 2, 3)),
            dma((2, 2, 3)),
            dma((2, 4, 5)),
            dma((2, 4, 5)),
            dma((NX, 2)),
            dma((NX, 2)),
            dma((2, 2, 2, 2)),
            dma((2, 2, 4, 2)),
            dma((2, 2, 4, 2)),
            dma((2, 2, 2, 2)),
        ],
        compiler_params=pltpu.CompilerParams(
            collective_id=0, has_side_effects=True, vmem_limit_bytes=66_000_000
        ),
        name="expert_backward",
    )(tokens, cotangent, w_up, w_down, expert_ids.T, gate_weights.T)
    token_grad, gates, down = pl.pallas_call(
        finish,
        out_shape=(
            jax.ShapeDtypeStruct(token_grad.shape, BF16),
            jax.ShapeDtypeStruct(gates.shape, BF16),
            jax.ShapeDtypeStruct(down.shape, F32),
        ),
        in_specs=[local] * 3,
        out_specs=[local] * 3,
        name="finish",
    )(token_grad, gates, down)
    return token_grad, gates.T, down[None]


def solution(mesh):
    return jax.shard_map(
        shards,
        mesh=mesh,
        in_specs=(
            P(("dp", "ep"), None),
            P(("dp", "ep"), None),
            P(("dp", "ep"), None),
            P(("dp", "ep"), None),
            P("ep", None, None),
            P("ep", None, None),
        ),
        out_specs=(P(("dp", "ep"), None), P(("dp", "ep"), None), P("ep", "dp", None)),
        check_vma=False,
    )
```

```python
import jax
import jax.numpy as jnp
from jax import lax
from jax.experimental import pallas as pl
from jax.experimental.pallas import tpu as pltpu
from jax.sharding import PartitionSpec as P

MESH = pl.DeviceIdType.MESH
BF16, F32 = jnp.bfloat16, jnp.float32
NX, NYH, NZ = 4, 4, 8
NY = 2 * NYH
ROWS = 128
LANES = 128
QUART = 512
EXP = 32
MID = 64


def kernel(
    x_ref, dy_ref, wu_ref, wd_ref, ids_ref, gates_ref, tok_ref, gg_ref, dg_ref,
    xb, db, gt, wu, wd, gh, gp, pre_s, bh_s, gs, gq, pb, pg, rb, rg, dyt, a1, a2, s1, s2, r1, r2, rx1, ry1, ry2, rx2,
    loc_sem, ag_send, ag_recv, w_send, w_recv, rs_send, rs_recv, c_send, c_recv, x_sems, y1_sems, y2_sems, x2_sems,
):
    width = dy_ref.shape[1]
    hid_n = wu_ref.shape[2]
    tile = width // NX
    dp, ep = lax.axis_index("dp"), lax.axis_index("ep")
    core = lax.rem(ep, 2)
    z = lax.rem(ep // 2, NZ)
    yl = ep // (2 * NZ)
    x, yh = dp // NYH, lax.rem(dp, NYH)
    yy = 2 * yh + yl

    def dev(x_, y_, z_, c_):
        return (x_ * NYH + y_ // 2, (lax.rem(y_, 2) * NZ + z_) * 2 + c_)

    zdev = [dev(x, yy, lax.rem(z + 1, NZ), core), dev(x, yy, lax.rem(z + NZ - 1, NZ), core)]
    cdev = dev(x, yy, z, 1 - core)
    ydev = [dev(x, lax.rem(yy + 1, NY), z, core), dev(x, lax.rem(yy + NY - 1, NY), z, core)]
    y_pair = dev(x, lax.rem(yy + NY + 1 - 2 * yl, NY), z, core)
    y_other = dev(x, lax.rem(yy + NY + 2 * yl - 1, NY), z, core)
    xdev = [dev(lax.rem(x + 1, NX), yy, z, core), dev(lax.rem(x + NX - 1, NX), yy, z, core)]

    barrier = pltpu.get_barrier_semaphore()
    partners = zdev + [cdev] + ydev + xdev
    for device in partners:
        pl.semaphore_signal(barrier, inc=1, device_id=device, device_id_type=MESH)

    OWN, FAR = (NZ - 2) * ROWS, (NZ - 1) * ROWS
    own = [
        pltpu.make_async_copy(x_ref, xb.at[pl.ds(OWN, ROWS)], loc_sem.at[0]),
        pltpu.make_async_copy(dy_ref, db.at[pl.ds(OWN, ROWS)], loc_sem.at[1]),
        pltpu.make_async_copy(wu_ref.at[0], wu.at[:, pl.ds(0, hid_n)], loc_sem.at[2]),
        pltpu.make_async_copy(wd_ref.at[0], wd.at[:, pl.ds(0, hid_n)], loc_sem.at[3]),
    ]
    for copy in own:
        copy.start()
    names = lax.broadcasted_iota(jnp.int32, (EXP, ROWS), 0)
    dense = jnp.zeros((EXP, ROWS), F32)
    for k in range(ids_ref.shape[0]):
        dense = dense + jnp.where(ids_ref[k : k + 1, :] == names, gates_ref[k : k + 1, :].astype(F32), 0.0)
    gt[NZ - 2] = dense.astype(BF16)
    pl.semaphore_wait(barrier, len(partners))

    def remote(src, dst, ssem, rsem, device):
        return pltpu.make_async_remote_copy(
            src_ref=src, dst_ref=dst, send_sem=ssem, recv_sem=rsem,
            device_id=device, device_id_type=MESH,
        )

    bufs = (xb, db)
    last_way = (0, 1, 0)

    def block(arr, k):
        if arr == 2:
            return gt.at[k]
        return bufs[arr].at[pl.ds(k * ROWS, ROWS)]

    def slot(s, r):
        return NZ - 1 if s == 4 else 2 * (s - 1) + r

    sent = []

    def send_block(arr, r, s, src):
        copy = remote(src, block(arr, slot(s, r)), ag_send.at[arr, r, s - 1], ag_recv.at[arr, r, s], zdev[r])
        copy.start()
        sent.append(copy)

    def arrive(arr, s):
        for r in range(2):
            if s == 4 and last_way[arr] != r:
                continue
            here = block(arr, slot(s, r))
            remote(here, here, ag_send.at[arr, r, 0], ag_recv.at[arr, r, s], zdev[r]).wait_recv()
            if s < 3 or (s == 3 and last_way[arr] == r):
                send_block(arr, r, s + 1, here)

    for arr, src in ((0, x_ref), (1, dy_ref), (2, gt.at[NZ - 2])):
        for r in range(2):
            send_block(arr, r, 1, src)
    part = width // 2
    weight_first, weight_core, weight_relay = [], [], []
    for h in range(2):
        for m, (src, buf, far) in enumerate(((wu_ref, wu, y_pair), (wd_ref, wd, y_other))):
            rows = pl.ds(h * part, part)
            lanes = [pl.ds(j * hid_n, hid_n) for j in range(4)]
            weight_first.append(remote(
                src.at[0, rows], buf.at[rows, lanes[1]], w_send.at[m, h, 0], w_recv.at[m, h, 0], far))
            weight_core.append(remote(
                src.at[0, rows], buf.at[rows, lanes[2]], w_send.at[m, h, 1], w_recv.at[m, h, 1], cdev))
            weight_relay.append(remote(
                buf.at[rows, lanes[1]], buf.at[rows, lanes[3]], w_send.at[m, h, 2], w_recv.at[m, h, 2], cdev))
    for copy in weight_first + weight_core:
        copy.start()

    lane = lax.broadcasted_iota(jnp.int32, (1, LANES), 1)
    lane32 = lax.broadcasted_iota(jnp.int32, (1, EXP), 1)
    chunk = 32
    slots = [((yl if j % 2 == 0 else 1 - yl) * NZ + z) * 2 + (core if j < 2 else 1 - core) for j in range(4)]

    def compute(k, blocks, ready=None):
        base, size = k * ROWS, blocks * ROWS
        rows = pl.ds(base, size)
        for b in range(blocks):
            gs[pl.ds(b * ROWS, ROWS), :] = gt[k + b].astype(F32).T

        def hidden_part(n, carry):
            at = pl.ds(pl.multiple_of(n * 512, 512), 512)
            pre_s[:size, at] = jnp.dot(xb[rows, :], wu[:, at], preferred_element_type=F32)
            bh_s[:size, at] = jnp.dot(db[rows, :], wd[:, at], preferred_element_type=F32)
            return carry

        lax.fori_loop(0, 4 * hid_n // 512, hidden_part, 0)

        def piece(q, carry):
            at = pl.multiple_of(q * chunk, chunk)
            sub = pl.ds(at, chunk)
            big = pl.ds(pl.multiple_of(base + at, chunk), chunk)
            out = jnp.zeros((chunk, LANES), F32)
            for j in range(4):
                lanes = pl.ds(j * hid_n, hid_n)
                g = jnp.sum(jnp.where(lane32 == slots[j], gs[sub, :], 0.0), axis=1, keepdims=True)
                pre, bh = pre_s[sub, lanes], bh_s[sub, lanes]
                sig = 0.5 * jnp.tanh(0.5 * pre) + 0.5
                hidden = (pre * sig).astype(BF16).astype(F32)
                gate = jnp.sum(bh * hidden, axis=1, keepdims=True)
                slope = sig * (1.0 + pre * (1.0 - sig))
                gp[sub, lanes] = (g * bh * slope).astype(BF16)
                gh[big, lanes] = (g * hidden).astype(BF16)
                out = jnp.where(lane == slots[j], gate, out)
            gq[sub, :] = out
            return carry

        lax.fori_loop(0, size // chunk, piece, 0)
        for b in range(blocks):
            pg[k + b] = gq[pl.ds(b * ROWS, ROWS), :].T[:EXP, :].astype(BF16)

        def columns(t, carry):
            at = pl.ds(pl.multiple_of(t * 512, 512), 512)
            pb[rows, at] = lax.dot_general(
                gp[:size, :], wu[at, :], (((1,), (1,)), ((), ())), preferred_element_type=F32).astype(BF16)
            return carry

        if ready is None:
            lax.fori_loop(0, width // 512, columns, 0)
            return
        before = None
        for t in (0, 2, 1, 3):
            columns(t, 0)
            if before is not None:
                ready(before)
            before = t
        ready(before)

    def core_copy(q, part):
        src, dst = ((s1.at[q], r1.at[q]), (s2.at[:, q], r2.at[:, q]))[part]
        return remote(src, dst, c_send.at[q, part], c_recv.at[q, part], cdev)

    deep = NZ * ROWS // 2

    def down_tile(phase):
        def body(q, carry):
            d = jnp.where(q == 0, 2, jnp.where(q == 3, 0, jnp.where(q == 2, 3, 1)))
            at = pl.ds(pl.multiple_of(lax.rem(x + d, NX) * tile, tile), tile)
            for k in range(deep // ROWS):
                dyt[:, pl.ds(k * ROWS, ROWS)] = db[pl.ds(phase * deep + k * ROWS, ROWS), at].T
            rows = pl.ds(phase * deep, deep)
            for by_x, by_y, start in ((s1, s2, 2 * hid_n), (a1, a2, 0)):
                term = jnp.dot(dyt[...], gh[rows, pl.ds(start, 2 * hid_n)], preferred_element_type=F32)
                for jj in range(2):
                    for row in range(NYH):
                        top = row * ROWS
                        upper = term[top : top + MID, jj * hid_n : (jj + 1) * hid_n]
                        lower = term[top + MID : top + ROWS, jj * hid_n : (jj + 1) * hid_n]
                        k = lax.rem(2 * row + (yl if jj == 0 else 1 - yl) + NY - yy, NY)
                        if phase:
                            upper = upper + by_x[q, jj, row].astype(F32)
                            lower = lower + by_y[k, q].astype(F32)
                        by_x[q, jj, row] = upper.astype(BF16)
                        by_y[k, q] = lower.astype(BF16)
            if phase:
                for half in range(2):
                    core_copy(q, half).start()
            return carry
        return body

    cols = [pl.ds(c * QUART, QUART) for c in range(4)]
    GATES = 4
    back = (zdev[1], zdev[0])

    def rs_copy(r, t, h):
        k = slot(4 - t, r)
        if h == GATES:
            src, dst = pg.at[k], rg.at[r, t]
        else:
            src, dst = pb.at[pl.ds(k * ROWS, ROWS), cols[h]], rb.at[r, t, :, cols[h]]
        return remote(src, dst, rs_send.at[r, t, h], rs_recv.at[r, t, h], back[r])

    def rs_add(r, t, h):
        rs_copy(r, t - 1, h).wait_recv()
        k = slot(4 - t, r)
        if h == GATES:
            pg[k] = (pg[k].astype(F32) + rg[r, t - 1].astype(F32)).astype(BF16)
        else:
            row = pl.ds(k * ROWS, ROWS)
            pb[row, cols[h]] = (
                pb[row, cols[h]].astype(F32) + rb[r, t - 1, :, cols[h]].astype(F32)).astype(BF16)
        rs_copy(r, t, h).start()

    def rs_free(t):
        for c in range(2):
            for r in range(2):
                rs_add(r, t, 2 * (1 - r) + c)

    def rs_tied(t, parts=(0, 1)):
        for c in parts:
            for r in range(2):
                rs_add(r, t, 2 * r + c)
        if 1 in parts:
            for r in range(2):
                if t > 1 or r == 0:
                    rs_add(r, t, GATES)

    for arr in (0, 1, 2):
        arrive(arr, 1)
    for first, relay in zip(weight_first, weight_relay):
        first.wait_recv()
        relay.start()
    for copy in own:
        copy.wait()
    for copy in weight_core + weight_relay:
        copy.wait_recv()
    compute(NZ - 2, 1)
    arrive(0, 2)
    compute(0, 2)
    arrive(1, 2)
    arrive(2, 2)
    compute(2, 2)
    arrive(0, 3)
    lax.fori_loop(0, NX, down_tile(0), 0)
    arrive(1, 3)
    arrive(2, 3)
    compute(4, 2)
    for c in range(2):
        for r in range(2):
            rs_copy(r, 1, 2 * (1 - r) + c).start()
    rs_copy(1, 1, GATES).start()
    for arr in (0, 1, 2):
        arrive(arr, 4)
    compute(NZ - 1, 1, lambda t: rs_copy(t // 2, 0, t).start())
    rs_copy(0, 0, GATES).start()
    lax.fori_loop(0, 2, down_tile(1), 0)
    rs_free(2)
    lax.fori_loop(2, NX, down_tile(1), 0)

    def add_into(dst, *others):
        total = dst[...].astype(F32)
        for other in others:
            total = total + other[...].astype(F32)
        dst[...] = total.astype(BF16)

    class Ring:
        def __init__(self, n, piece, recv, sems, devices):
            self.n, self.piece, self.recv, self.sems, self.devices = n, piece, recv, sems, devices
            self.started = []

        def copy(self, r, t, h):
            m = self.n // 2 - t
            return remote(
                self.piece(m if r == 0 else self.n - m, h), self.recv.at[r, t, h],
                self.sems.at[0, r, t, h], self.sems.at[1, r, t, h], self.devices[r])

        def send(self, r, t, h):
            self.copy(r, t, h).start()
            self.started.append((r, t, h))

        def begin(self):
            for r in range(2):
                self.send(r, 0, r)

        def forward(self, t, free):
            for r in range(2):
                h = 1 - r if free else r
                if t > 1 or not free:
                    m = self.n // 2 - t
                    self.copy(r, t - 1, h).wait_recv()
                    add_into(self.piece(m if r == 0 else self.n - m, h), self.recv.at[r, t - 1, h])
                self.send(r, t, h)

        def finish(self):
            t = self.n // 2 - 1
            for free in (1, 0):
                for r in range(2):
                    self.copy(r, t, 1 - r if free else r).wait_recv()
            for h in range(2):
                add_into(self.piece(0, h), self.recv.at[0, t, h], self.recv.at[1, t, h])

        def drain(self):
            for r, t, h in self.started:
                self.copy(r, t, h).wait_send()

    place = {2: 0, 1: 1, NX - 1: 2, 0: 3}
    sub = MID // 2

    def y_row(k):
        return lax.rem(yy + k, NY) // 2

    ring_x1 = Ring(NX, lambda k, h: a1.at[place[k], h], rx1, x_sems, xdev)
    ring_y1 = Ring(NY, lambda k, h: a1.at[3, k % 2, y_row(k), pl.ds(h * sub, sub)], ry1, y1_sems, ydev)
    ring_y2 = Ring(NY, lambda k, h: a2.at[k, pl.ds(2 * h, 2)], ry2, y2_sems, ydev)
    ring_x2 = Ring(NX, lambda k, h: a2.at[0, place[k], pl.ds(h * sub, sub)], rx2, x2_sems, xdev)

    for q in range(3):
        core_copy(q, 0).wait_recv()
        for jj in range(2):
            add_into(a1.at[q, jj], r1.at[q, jj])
        if q == 0:
            ring_x1.begin()
    ring_x1.forward(1, True)
    for q in range(NX):
        core_copy(q, 1).wait_recv()
    for k in (NY // 2, 3, 5):
        add_into(a2.at[k], r2.at[k])
        if k == NY // 2:
            ring_y2.begin()
    ring_y2.forward(1, True)
    rs_tied(1)
    for k in (2, 6, 1, 7, 0):
        add_into(a2.at[k], r2.at[k])
    core_copy(3, 0).wait_recv()
    for jj in range(2):
        add_into(a1.at[3, jj], r1.at[3, jj])
    ring_y2.forward(1, False)
    ring_x1.forward(1, False)
    ring_y2.forward(2, True)
    rs_free(3)
    ring_y2.forward(2, False)
    rs_tied(2, (0,))
    ring_y2.forward(3, True)
    rs_tied(2, (1,))
    ring_x1.finish()
    ring_y1.begin()
    ring_y1.forward(1, True)
    ring_y2.forward(3, False)
    ring_y1.forward(2, True)
    ring_y1.forward(1, False)
    rs_tied(3, (0,))
    ring_y2.finish()
    ring_x2.begin()
    ring_x2.forward(1, True)
    ring_y1.forward(3, True)
    ring_y1.forward(2, False)
    rs_tied(3, (1,))
    ring_x2.forward(1, False)
    ring_y1.forward(3, False)
    ring_x2.finish()
    dg_ref[MID:, :] = a2[0, 3].astype(F32)
    ring_y1.finish()
    dg_ref[:MID, :] = a1[3, 0, yh].astype(F32)

    mine = pl.ds(OWN, ROWS)
    for h in (0, 2, 1, 3):
        for r in range(2):
            rs_copy(r, 3, h).wait_recv()
        tok_ref[:, cols[h]] = (
            pb[mine, cols[h]].astype(F32) + rb[0, 3, :, cols[h]].astype(F32) + rb[1, 3, :, cols[h]].astype(F32)
        ).astype(BF16)
    for r in range(2):
        rs_copy(r, 3, GATES).wait_recv()
    gates = pg[NZ - 2].astype(F32) + rg[0, 3].astype(F32) + rg[1, 3].astype(F32)
    for k in range(ids_ref.shape[0]):
        picked = jnp.where(ids_ref[k : k + 1, :] == names, gates, 0.0)
        gg_ref[k : k + 1, :] = jnp.sum(picked, axis=0, keepdims=True)

    for copy in sent + weight_first + weight_core + weight_relay:
        copy.wait_send()
    for r in range(2):
        for t in range(4):
            for h in range(5):
                if t == 0 and h not in ((0, 1, GATES) if r == 0 else (2, 3)):
                    continue
                rs_copy(r, t, h).wait_send()
    for q in range(NX):
        for half in range(2):
            core_copy(q, half).wait_send()
    for ring in (ring_x1, ring_y1, ring_y2, ring_x2):
        ring.drain()


def finish(tok_ref, gates_ref, down_ref, tok_out, gates_out, down_out):
    tok_out[...] = tok_ref[...]
    gates_out[...] = gates_ref[...].astype(BF16)
    down_out[...] = down_ref[...]


def shards(tokens, cotangent, expert_ids, gate_weights, w_up, w_down):
    rows, width = tokens.shape
    hid_n = w_up.shape[2]
    tile = width // NX
    dma, vmem = pltpu.SemaphoreType.DMA, pltpu.VMEM
    hbm = pl.BlockSpec(memory_space=pl.ANY)
    local = pl.BlockSpec(memory_space=pltpu.VMEM)
    token_grad, gates, down = pl.pallas_call(
        kernel,
        out_shape=(
            jax.ShapeDtypeStruct((rows, width), BF16),
            jax.ShapeDtypeStruct((expert_ids.shape[1], rows), F32),
            jax.ShapeDtypeStruct((width // (NX * NYH), hid_n), F32),
        ),
        in_specs=[hbm] * 4 + [local] * 2,
        out_specs=[local] * 3,
        scratch_shapes=[
            vmem((NZ * rows, width), BF16),
            vmem((NZ * rows, width), BF16),
            vmem((NZ, EXP, rows), BF16),
            vmem((width, 4 * hid_n), BF16),
            vmem((width, 4 * hid_n), BF16),
            vmem((NZ * rows, 4 * hid_n), BF16),
            vmem((2 * rows, 4 * hid_n), BF16),
            vmem((2 * rows, 4 * hid_n), F32),
            vmem((2 * rows, 4 * hid_n), F32),
            vmem((2 * rows, EXP), F32),
            vmem((2 * rows, LANES), F32),
            vmem((NZ * rows, width), BF16),
            vmem((NZ, EXP, rows), BF16),
            vmem((2, 4, rows, width), BF16),
            vmem((2, 4, EXP, rows), BF16),
            vmem((tile, NZ * rows // 2), BF16),
            vmem((NX, 2, NYH, MID, hid_n), BF16),
            vmem((NY, NX, MID, hid_n), BF16),
            vmem((NX, 2, NYH, MID, hid_n), BF16),
            vmem((NY, NX, MID, hid_n), BF16),
            vmem((NX, 2, NYH, MID, hid_n), BF16),
            vmem((NY, NX, MID, hid_n), BF16),
            vmem((2, 2, 2, NYH, MID, hid_n), BF16),
            vmem((2, 4, 2, MID // 2, hid_n), BF16),
            vmem((2, 4, 2, 2, MID, hid_n), BF16),
            vmem((2, 2, 2, MID // 2, hid_n), BF16),
            dma((4,)),
            dma((3, 2, 4)),
            dma((3, 2, 5)),
            dma((2, 2, 3)),
            dma((2, 2, 3)),
            dma((2, 4, 5)),
            dma((2, 4, 5)),
            dma((NX, 2)),
            dma((NX, 2)),
            dma((2, 2, 2, 2)),
            dma((2, 2, 4, 2)),
            dma((2, 2, 4, 2)),
            dma((2, 2, 2, 2)),
        ],
        compiler_params=pltpu.CompilerParams(
            collective_id=0, has_side_effects=True, vmem_limit_bytes=66_000_000
        ),
        name="expert_backward",
    )(tokens, cotangent, w_up, w_down, expert_ids.T, gate_weights.T)
    token_grad, gates, down = pl.pallas_call(
        finish,
        out_shape=(
            jax.ShapeDtypeStruct(token_grad.shape, BF16),
            jax.ShapeDtypeStruct(gates.shape, BF16),
            jax.ShapeDtypeStruct(down.shape, F32),
        ),
        in_specs=[local] * 3,
        out_specs=[local] * 3,
        name="finish",
    )(token_grad, gates, down)
    return token_grad, gates.T, down[None]


def solution(mesh):
    return jax.shard_map(
        shards,
        mesh=mesh,
        in_specs=(
            P(("dp", "ep"), None),
            P(("dp", "ep"), None),
            P(("dp", "ep"), None),
            P(("dp", "ep"), None),
            P("ep", None, None),
            P("ep", None, None),
        ),
        out_specs=(P(("dp", "ep"), None), P(("dp", "ep"), None), P("ep", "dp", None)),
        check_vma=False,
    )
```
